768 devices in a mesh: fsdp: 96 (over z, x, core), tensor: 8 (over y).
Axes of the slice: x: 4, y: 8, z: 12, core: 2. Of those that a mesh axis runs over, the one named last changes fastest.
Arguments:
- momentum: float32 [23040, 6144], P('fsdp', 'tensor'), may hold values from -100 to 100
- gradient: bfloat16 [23040, 6144], P('fsdp', 'tensor'), may hold values from -3 to 3
- right_basis: float32 [6144, 512], P('tensor'), may hold values from -0.078125 to 0.078125
Outputs:
- update: bfloat16 [23040, 6144], P('fsdp', 'tensor')
- new_momentum: float32 [23040, 6144], P('fsdp', 'tensor')
- left_scaled: float32 [23040, 512], P('fsdp')
- next_basis: float32 [6144, 512], P(('tensor', 'fsdp'))
The draws below stay inside these ranges and needn't reach their ends.
All inputs are finite; a program needn't handle non-finite values.
Results may differ from the reference program's by a relative error of at most 0.001.
Values sent between devices are 32-bit elements; how exact they have to be, the bound alone decides.
A program may use at most 32 MiB of HBM per device.

```python
import math
import jax
import jax.numpy as jnp
from jax import lax

RANK = 512
N = 6144
M = 23040


def draw_momentum(key, part):
    key_noise, key_rows, key_cols = jax.random.split(key, 3)
    rising = jnp.exp(math.log(3.0) * jnp.arange(M, dtype=jnp.float32) / M)
    col_rising = jnp.exp(math.log(3.0) * jnp.arange(N, dtype=jnp.float32) / N)
    col_scale = col_rising * jnp.exp(jax.random.uniform(key_cols, (N,), jnp.float32, 0.0, math.log(10.0)))
    row_scale = jnp.exp(jax.random.uniform(key_rows, (M,), jnp.float32, 0.0, math.log(10.0)))
    noise = jnp.clip(jax.random.normal(key_noise, (M, N), jnp.float32), -4.0, 4.0)
    return 0.02 * (rising * row_scale)[:, None] * col_scale[None, :] * noise


def block_levels(own_key, dims, cuts, smallest, top_value):
    level, own = 1.0, jax.random.fold_in(own_key, 6)
    for axis_at, shards_of in cuts:
        draws = jnp.exp(jax.random.uniform(jax.random.fold_in(own, axis_at), (shards_of,), jnp.float32, smallest / len(cuts), top_value / len(cuts)))
        level = level * jnp.repeat(draws, dims[axis_at] // shards_of).reshape([-1 if axis == axis_at else 1 for axis in range(len(dims))])
    return level


def gaussian(stream_key, dims, deviation, bound, pieces=(), held_as=jnp.bfloat16):
    factor_of = block_levels(stream_key, dims, pieces, -0.22, 0.18) if pieces else 1.0
    entries = jax.random.normal(stream_key, dims, jnp.float32) * deviation * factor_of
    return jnp.minimum(jnp.maximum(entries, -bound), bound).astype(held_as)


def setup_inputs(seed: int = 0) -> dict:
    arg_keys = jax.random.split(jax.random.key(seed), 4)
    return {
        "momentum": draw_momentum(jax.random.fold_in(arg_keys[3], 71), 0),
        "gradient": gaussian(arg_keys[1], (M, N), 0.5, 3.0, ((0, 96), (1, 8))),
        "right_basis": gaussian(arg_keys[2], (N, RANK), N ** -0.5, 0.078125, ((0, 8),), jnp.float32),
    }


def reference(momentum, gradient, right_basis):
    highest = lax.Precision.HIGHEST
    summed = momentum + gradient.astype(jnp.float32)
    left_raw = jnp.dot(summed, right_basis, precision=highest)
    gram = jnp.dot(left_raw.T, left_raw, precision=highest)
    factor_lower = jnp.linalg.cholesky(gram)
    left = jax.scipy.linalg.solve_triangular(factor_lower, left_raw.T, lower=True).T
    right_factor = jnp.dot(summed.T, left, precision=highest)
    column_norm = jnp.sqrt(lax.optimization_barrier(jnp.sum(right_factor * right_factor, axis=0)) + 1e-06)
    next_basis = right_factor / column_norm[None, :]
    scaled_left = left * (math.sqrt(M / N) / column_norm)[None, :]
    update = jnp.dot(scaled_left, right_factor.T, precision=highest).astype(jnp.bfloat16)
    product = jnp.dot(left, right_factor.T, precision=highest)
    new_momentum = summed - 0.5 * product
    return (update, new_momentum, left * math.sqrt(M), next_basis)
```

```python
import functools
import math

import jax
import jax.numpy as jnp
from jax import lax
from jax.experimental import pallas as pl
from jax.experimental.pallas import tpu as pltpu
from jax.sharding import PartitionSpec as P

EPSILON = 1e-06
HIGHEST = lax.Precision.HIGHEST
MESH = pl.DeviceIdType.MESH
XS, CORES = 4, 2
VMEM_LIMIT = 60 * 1024 * 1024


def dot(a, b, lhs=1, rhs=0):
    return lax.dot_general(
        a, b, (((lhs,), (rhs,)), ((), ())), precision=HIGHEST, preferred_element_type=jnp.float32
    )


def place():
    f = lax.axis_index("fsdp")
    y = lax.axis_index("tensor")
    return f // (XS * CORES), (f // CORES) % XS, f % CORES, y


def device(z, x, core, y):
    return ((z * XS + x) * CORES + core, y)


def each(start, stop, body):
    def step(i, carry):
        body(i)
        return carry

    lax.fori_loop(start, stop, step, 0)


def reduce_kernel(
    zs_n, ys_n, m_ref, g_ref, q_ref, a_ref, w_ref, gram_ref,
    part, ybuf, chunks, wpart, gpart, cbuf, xsum, xbuf, zsum, zbuf, zgbuf, wfull, gfull,
    s_y, r_y, s_y2, r_y2, s_c, r_c, s_x, r_x, s_z, r_z, s_zg, r_zg, s_gy, r_gy, s_gx, r_gx, s_gc, r_gc,
    s_wz, r_wz, s_wx, r_wx, s_wc, r_wc,
):
    z, x, core, y = place()
    half = part.shape[1]
    lanes = part.shape[2]
    across = a_ref.shape[1] // lanes

    def send(src, dst, ssem, rsem, to):
        pltpu.make_async_remote_copy(
            src_ref=src, dst_ref=dst, send_sem=ssem, recv_sem=rsem, device_id=to, device_id_type=MESH
        ).start()

    def sent(src, ssem):
        pltpu.make_async_copy(src, src, ssem).wait()

    def came(dst, rsem):
        pltpu.make_async_copy(dst, dst, rsem).wait()

    barrier = pltpu.get_barrier_semaphore()

    def greet(to):
        pl.semaphore_signal(barrier, inc=1, device_id=to, device_id_type=MESH)

    each(1, ys_n, lambda d: greet(device(z, x, core, (y + d) % ys_n)))
    greet(device(z, x, 1 - core, y))
    each(1, XS, lambda d: greet(device(z, (x + d) % XS, core, y)))
    each(1, zs_n, lambda d: greet(device((z + d) % zs_n, x, core, y)))

    summed = m_ref[...] + g_ref[...].astype(jnp.float32)
    left_part = dot(summed, q_ref[...])
    for k in range(ys_n):
        row, col = k // across, k % across
        part[k] = left_part[row * half : (row + 1) * half, col * lanes : (col + 1) * lanes]
    pl.semaphore_wait(barrier, (ys_n - 1) + 1 + (XS - 1) + (zs_n - 1))

    def y_of(d):
        return (y + d) % ys_n

    each(1, ys_n, lambda d: send(part.at[y_of(d)], ybuf.at[y], s_y.at[d], r_y.at[y], device(z, x, core, y_of(d))))
    ybuf[y] = part[y]
    each(1, ys_n, lambda d: came(ybuf.at[y_of(d)], r_y.at[y_of(d)]))
    total = ybuf[0]
    for k in range(1, ys_n):
        total = total + ybuf[k]
    chunks[y] = total
    each(1, ys_n, lambda d: send(chunks.at[y], chunks.at[y], s_y2.at[d], r_y2.at[y], device(z, x, core, y_of(d))))
    each(1, ys_n, lambda d: came(chunks.at[y_of(d)], r_y2.at[y_of(d)]))
    for k in range(ys_n):
        row, col = k // across, k % across
        a_ref[row * half : (row + 1) * half, col * lanes : (col + 1) * lanes] = chunks[k]

    left_raw = a_ref[...]
    wpart[0:zs_n] = dot(summed, left_raw, 0, 0).reshape(zs_n, XS, CORES, 8, -1)
    gpart[...] = dot(left_raw, left_raw, 0, 0).reshape(gpart.shape)
    wpart[zs_n] = gpart[y]

    def x_of(d):
        return (x + d) % XS

    def z_of(d):
        return (z + d) % zs_n

    partner = device(z, x, 1 - core, y)
    each(1, XS + 1, lambda d: send(
        wpart.at[:, x_of(d), 1 - core], cbuf.at[x_of(d)], s_c.at[d - 1], r_c.at[x_of(d)], partner))

    def forward(d):
        k = x_of(d)
        came(cbuf.at[k], r_c.at[k])
        xsum[k] = wpart[:, k, core] + cbuf[k]
        send(xsum.at[k], xbuf.at[x], s_x.at[d], r_x.at[x], device(z, k, core, y))

    each(1, XS, forward)
    came(cbuf.at[x], r_c.at[x])
    xbuf[x] = wpart[:, x, core] + cbuf[x]
    each(1, XS, lambda d: came(xbuf.at[x_of(d)], r_x.at[x_of(d)]))
    zsum[...] = (xbuf[0] + xbuf[1]) + (xbuf[2] + xbuf[3])
    each(1, zs_n, lambda d: send(zsum.at[zs_n], zgbuf.at[z], s_zg.at[d], r_zg.at[z], device(z_of(d), x, core, y)))
    each(1, zs_n, lambda d: send(zsum.at[z_of(d)], zbuf.at[z], s_z.at[d], r_z.at[z], device(z_of(d), x, core, y)))
    zgbuf[z] = zsum[zs_n]
    zbuf[z] = zsum[z]

    each(1, zs_n, lambda d: came(zgbuf.at[z_of(d)], r_zg.at[z_of(d)]))
    tile = zgbuf[0]
    for k in range(1, zs_n):
        tile = tile + zgbuf[k]
    gfull[y, x, core] = tile
    mine = gfull.at[y, x, core]
    each(1, ys_n, lambda d: send(mine, mine, s_gy.at[d], r_gy.at[y], device(z, x, core, y_of(d))))

    each(1, zs_n, lambda d: came(zbuf.at[z_of(d)], r_z.at[z_of(d)]))
    tile = zbuf[0]
    for k in range(1, zs_n):
        tile = tile + zbuf[k]
    wfull[z, x, core] = tile
    own = wfull.at[z, x, core]
    each(1, zs_n, lambda d: send(own, own, s_wz.at[d], r_wz.at[z], device(z_of(d), x, core, y)))

    each(1, ys_n, lambda d: came(gfull.at[y_of(d), x, core], r_gy.at[y_of(d)]))
    gx = gfull.at[:, x, core]
    each(1, XS, lambda d: send(gx, gx, s_gx.at[d], r_gx.at[x], device(z, x_of(d), core, y)))
    each(1, zs_n, lambda d: came(wfull.at[z_of(d), x, core], r_wz.at[z_of(d)]))
    wx = wfull.at[:, x, core]
    each(1, XS, lambda d: send(wx, wx, s_wx.at[d], r_wx.at[x], device(z, x_of(d), core, y)))

    each(1, XS, lambda d: came(gfull.at[:, x_of(d), core], r_gx.at[x_of(d)]))
    gc = gfull.at[:, :, core]
    send(gc, gc, s_gc, r_gc, partner)
    each(1, XS, lambda d: came(wfull.at[:, x_of(d), core], r_wx.at[x_of(d)]))
    wc = wfull.at[:, :, core]
    send(wc, wc, s_wc, r_wc, partner)
    came(gfull.at[:, :, 1 - core], r_gc)
    gram_ref[...] = gfull[...].reshape(gram_ref.shape)
    came(wfull.at[:, :, 1 - core], r_wc)
    w_ref[...] = wfull[...].reshape(w_ref.shape)

    def drain_y(d):
        sent(part.at[y_of(d)], s_y.at[d])
        sent(chunks.at[y], s_y2.at[d])
        sent(mine, s_gy.at[d])

    def drain_x(d):
        sent(xsum.at[x_of(d)], s_x.at[d])
        sent(gx, s_gx.at[d])
        sent(wx, s_wx.at[d])

    def drain_z(d):
        sent(zsum.at[zs_n], s_zg.at[d])
        sent(zsum.at[z_of(d)], s_z.at[d])
        sent(own, s_wz.at[d])

    each(1, ys_n, drain_y)
    each(1, XS, drain_x)
    each(1, zs_n, drain_z)
    each(1, XS + 1, lambda d: sent(wpart.at[:, x_of(d), 1 - core], s_c.at[d - 1]))
    sent(gc, s_gc)
    sent(wc, s_wc)


def reduce_all(zs_n, ys_n, momentum, gradient, right_basis):
    rows, cols = momentum.shape
    rank = right_basis.shape[1]
    f32 = jnp.float32
    lanes = 128
    half = rows * rank // (ys_n * lanes)
    sems = []
    for n in (ys_n, ys_n, XS, XS, zs_n, zs_n, ys_n, XS):
        sems += [pltpu.SemaphoreType.DMA((n,))] * 2
    sems += [pltpu.SemaphoreType.DMA] * 2
    for n in (zs_n, XS):
        sems += [pltpu.SemaphoreType.DMA((n,))] * 2
    sems += [pltpu.SemaphoreType.DMA] * 2
    vmem = pl.BlockSpec(memory_space=pltpu.VMEM)
    return pl.pallas_call(
        functools.partial(reduce_kernel, zs_n, ys_n),
        name="reduce_all",
        out_shape=(
            jax.ShapeDtypeStruct((rows, rank), f32),
            jax.ShapeDtypeStruct((cols, rank), f32),
            jax.ShapeDtypeStruct((rank, rank), f32),
        ),
        in_specs=[vmem] * 3,
        out_specs=(vmem,) * 3,
        scratch_shapes=[
            pltpu.VMEM((ys_n, half, lanes), f32),
            pltpu.VMEM((ys_n, half, lanes), f32),
            pltpu.VMEM((ys_n, half, lanes), f32),
            pltpu.VMEM((zs_n + 1, XS, CORES, 8, rank), f32),
            pltpu.VMEM((ys_n, XS, CORES, 8, rank), f32),
            pltpu.VMEM((XS, zs_n + 1, 8, rank), f32),
            pltpu.VMEM((XS, zs_n + 1, 8, rank), f32),
            pltpu.VMEM((XS, zs_n + 1, 8, rank), f32),
            pltpu.VMEM((zs_n + 1, 8, rank), f32),
            pltpu.VMEM((zs_n, 8, rank), f32),
            pltpu.VMEM((zs_n, 8, rank), f32),
            pltpu.VMEM((zs_n, XS, CORES, 8, rank), f32),
            pltpu.VMEM((ys_n, XS, CORES, 8, rank), f32),
            *sems,
        ],
        compiler_params=pltpu.CompilerParams(
            collective_id=0, has_side_effects=True, vmem_limit_bytes=VMEM_LIMIT
        ),
    )(momentum, gradient, right_basis)


BLOCK = 128


def factor_block(tiles):
    shape = (8, BLOCK)
    lane = lax.broadcasted_iota(jnp.int32, shape, 1)
    sub = lax.broadcasted_iota(jnp.int32, shape, 0)
    count = len(tiles)
    out = []

    def column(tile, k):
        return jnp.broadcast_to(tile[:, k : k + 1], shape)

    def row(tile, k):
        return jnp.broadcast_to(tile[k : k + 1, :], shape)

    tiles = list(tiles)
    for t in range(count):
        base = 8 * t
        here = (lane >= base) & (lane < base + 8)
        tile = tiles[t]
        cols = [column(tile, base + c) for c in range(8)]
        start = jnp.where(here, jnp.where(lane - base == sub, 1.0, 0.0), tile)
        scale, rows, low = [], [], {}
        for p in range(8):
            r = lax.rsqrt(row(cols[p], p))
            lp = cols[p] * r
            for c in range(p + 1, 8):
                low[p, c] = row(lp, c)
                cols[c] = cols[c] - lp * low[p, c]
            w = row(start, p)
            for q in range(p):
                w = w - low[q, p] * rows[q]
            rows.append(w * r)
            scale.append(r)
        done = rows[7]
        for p in range(7):
            done = jnp.where(sub == p, rows[p], done)
        out.append(jnp.where(lane < base + 8, done, 0.0))
        if t + 1 == count:
            break
        solved = [None] * 8
        for p in reversed(range(8)):
            w = rows[p]
            for q in range(p + 1, 8):
                w = w - low[p, q] * solved[q]
            solved[p] = w * scale[p]
        for i in range(t + 1, count):
            acc = jnp.where(here, 0.0, tiles[i])
            for p in range(8):
                acc = acc - column(tiles[i], base + p) * solved[p]
            tiles[i] = acc
    return out


def factor_kernel(gram_ref, inv_ref, work, diag):
    size = gram_ref.shape[0]
    work[...] = gram_ref[...]
    inv_ref[...] = jnp.zeros_like(inv_ref)
    lane = lax.broadcasted_iota(jnp.int32, (BLOCK, size), 1)

    @pl.loop(0, size // BLOCK)
    def _(b):
        off = pl.multiple_of(b * BLOCK, BLOCK)
        here = pl.ds(off, BLOCK)
        tiles = [work[pl.ds(pl.multiple_of(off + 8 * i, 8), 8), here] for i in range(BLOCK // 8)]
        for i, tile in enumerate(factor_block(tiles)):
            diag[8 * i : 8 * i + 8, :] = tile
        top = diag[...]
        inv_ref[here, :] = dot(top, inv_ref[here, :])
        inv_ref[here, here] = top

        @pl.when(b + 1 < size // BLOCK)
        def _():
            panel = jnp.where(lane >= off + BLOCK, dot(top, work[here, :]), 0.0)[:, BLOCK:]
            work[BLOCK:, BLOCK:] = work[BLOCK:, BLOCK:] - dot(panel, panel, 0, 0)
            inv_ref[BLOCK:, :] = inv_ref[BLOCK:, :] - dot(panel, inv_ref[here, :], 0, 0)


def factor(gram):
    vmem = pl.BlockSpec(memory_space=pltpu.VMEM)
    return pl.pallas_call(
        factor_kernel,
        name="factor",
        out_shape=jax.ShapeDtypeStruct(gram.shape, jnp.float32),
        in_specs=[vmem],
        out_specs=vmem,
        scratch_shapes=[pltpu.VMEM(gram.shape, jnp.float32), pltpu.VMEM((BLOCK, BLOCK), jnp.float32)],
        compiler_params=pltpu.CompilerParams(vmem_limit_bytes=VMEM_LIMIT),
    )(gram)


def finish_kernel(
    ys_n, total_rows, factor_value, m_ref, g_ref, a_ref, w_ref, inv_ref,
    update_ref, momentum_ref, left_ref, basis_ref, right, norms, s_n, r_n,
):
    z, x, core, y = place()
    barrier = pltpu.get_barrier_semaphore()

    def peer(d):
        return device(z, x, core, (y + d) % ys_n)

    each(1, ys_n, lambda d: pl.semaphore_signal(barrier, inc=1, device_id=peer(d), device_id_type=MESH))
    inverse = inv_ref[...]
    right[...] = dot(w_ref[...], inverse, 1, 1)
    values = right[...]
    norms[y] = jnp.sum(values * values, axis=0, keepdims=True)
    pl.semaphore_wait(barrier, ys_n - 1)

    def copy(d, slot):
        return pltpu.make_async_remote_copy(
            src_ref=norms.at[slot], dst_ref=norms.at[slot], send_sem=s_n.at[d], recv_sem=r_n.at[slot],
            device_id=peer(d), device_id_type=MESH,
        )

    each(1, ys_n, lambda d: copy(d, y).start())
    left = dot(a_ref[...], inverse, 1, 1)
    left_ref[...] = left * math.sqrt(total_rows)
    summed = m_ref[...] + g_ref[...].astype(jnp.float32)
    momentum_ref[...] = summed - 0.5 * dot(left, values, 1, 1)
    each(1, ys_n, lambda d: copy(d, (y + d) % ys_n).wait_recv())
    total = norms[0]
    for k in range(1, ys_n):
        total = total + norms[k]
    column_norm = jnp.sqrt(total + EPSILON)
    scaled = left * (factor_value / column_norm)
    update_ref[...] = dot(scaled, values, 1, 1).astype(update_ref.dtype)
    me = pl.multiple_of(lax.axis_index("fsdp") * 8, 8)
    basis_ref[...] = right[pl.ds(me, 8), :] / column_norm
    each(1, ys_n, lambda d: copy(d, y).wait_send())


def finish(ys_n, total_rows, factor_value, momentum, gradient, left_raw, w, inverse):
    rows, cols = momentum.shape
    rank = w.shape[1]
    f32 = jnp.float32
    vmem = pl.BlockSpec(memory_space=pltpu.VMEM)
    return pl.pallas_call(
        functools.partial(finish_kernel, ys_n, total_rows, factor_value),
        name="finish",
        out_shape=(
            jax.ShapeDtypeStruct((rows, cols), jnp.bfloat16),
            jax.ShapeDtypeStruct((rows, cols), f32),
            jax.ShapeDtypeStruct((rows, rank), f32),
            jax.ShapeDtypeStruct((8, rank), f32),
        ),
        in_specs=[vmem] * 5,
        out_specs=(vmem,) * 4,
        scratch_shapes=[
            pltpu.VMEM((cols, rank), f32),
            pltpu.VMEM((ys_n, 1, rank), f32),
            pltpu.SemaphoreType.DMA((ys_n,)),
            pltpu.SemaphoreType.DMA((ys_n,)),
        ],
        compiler_params=pltpu.CompilerParams(
            collective_id=1, has_side_effects=True, vmem_limit_bytes=VMEM_LIMIT
        ),
    )(momentum, gradient, left_raw, w, inverse)


def on_device(momentum, gradient, right_basis):
    groups = lax.axis_size("fsdp")
    ys_n = lax.axis_size("tensor")
    zs_n = groups // (XS * CORES)
    left_raw, w, gram = reduce_all(zs_n, ys_n, momentum, gradient, right_basis)
    inverse = factor(gram)
    total_rows = momentum.shape[0] * groups
    total_cols = momentum.shape[1] * ys_n
    ratio = math.sqrt(total_rows / total_cols)
    return finish(ys_n, total_rows, ratio, momentum, gradient, left_raw, w, inverse)


def solution(mesh):
    in_specs = (P("fsdp", "tensor"), P("fsdp", "tensor"), P("tensor", None))
    out_specs = (
        P("fsdp", "tensor"),
        P("fsdp", "tensor"),
        P("fsdp", None),
        P(("tensor", "fsdp"), None),
    )
    return jax.shard_map(
        on_device, mesh=mesh, in_specs=in_specs, out_specs=out_specs, check_vma=False
    )
```

```python
import functools
import math

import jax
import jax.numpy as jnp
from jax import lax
from jax.experimental import pallas as pl
from jax.experimental.pallas import tpu as pltpu
from jax.sharding import PartitionSpec as P

EPSILON = 1e-06
HIGHEST = lax.Precision.HIGHEST
MESH = pl.DeviceIdType.MESH
XS, CORES = 4, 2
VMEM_LIMIT = 60 * 1024 * 1024


def dot(a, b, lhs=1, rhs=0):
    return lax.dot_general(
        a, b, (((lhs,), (rhs,)), ((), ())), precision=HIGHEST, preferred_element_type=jnp.float32
    )


def split(a):
    high = a.astype(jnp.bfloat16)
    return high, (a - high.astype(jnp.float32)).astype(jnp.bfloat16)


def dot3(a, b, lhs=1, rhs=0):
    def one(p, q):
        return lax.dot_general(p, q, (((lhs,), (rhs,)), ((), ())), preferred_element_type=jnp.float32)

    return one(a[0], b[0]) + (one(a[0], b[1]) + one(a[1], b[0]))


def place():
    f = lax.axis_index("fsdp")
    y = lax.axis_index("tensor")
    return f // (XS * CORES), (f // CORES) % XS, f % CORES, y


def device(z, x, core, y):
    return ((z * XS + x) * CORES + core, y)


def each(start, stop, body):
    def step(i, carry):
        body(i)
        return carry

    lax.fori_loop(start, stop, step, 0)


BLOCK = 128


def factor_block(tiles):
    shape = (8, BLOCK)
    lane = lax.broadcasted_iota(jnp.int32, shape, 1)
    sub = lax.broadcasted_iota(jnp.int32, shape, 0)
    count = len(tiles)
    out = []

    def column(tile, k):
        return jnp.broadcast_to(tile[:, k : k + 1], shape)

    def row(tile, k):
        return jnp.broadcast_to(tile[k : k + 1, :], shape)

    tiles = list(tiles)
    for t in range(count):
        base = 8 * t
        here = (lane >= base) & (lane < base + 8)
        tile = tiles[t]
        cols = [column(tile, base + c) for c in range(8)]
        start = jnp.where(here, jnp.where(lane - base == sub, 1.0, 0.0), tile)
        scale, rows, low = [], [], {}
        for p in range(8):
            r = lax.rsqrt(row(cols[p], p))
            lp = cols[p] * r
            for c in range(p + 1, 8):
                low[p, c] = row(lp, c)
                cols[c] = cols[c] - lp * low[p, c]
            w = row(start, p)
            for q in range(p):
                w = w - low[q, p] * rows[q]
            rows.append(w * r)
            scale.append(r)
        done = rows[7]
        for p in range(7):
            done = jnp.where(sub == p, rows[p], done)
        out.append(jnp.where(lane < base + 8, done, 0.0))
        if t + 1 == count:
            break
        solved = [None] * 8
        for p in reversed(range(8)):
            w = rows[p]
            for q in range(p + 1, 8):
                w = w - low[p, q] * solved[q]
            solved[p] = w * scale[p]
        for i in range(t + 1, count):
            acc = jnp.where(here, 0.0, tiles[i])
            for p in range(8):
                acc = acc - column(tiles[i], base + p) * solved[p]
            tiles[i] = acc
    return out


def factor_step(b, work, top_ref, between):
    size = work.shape[0]
    off = pl.multiple_of(b * BLOCK, BLOCK)
    here = pl.ds(off, BLOCK)
    tiles = [work[pl.ds(pl.multiple_of(off + 8 * i, 8), 8), here] for i in range(BLOCK // 8)]
    for i, tile in enumerate(factor_block(tiles)):
        top_ref[8 * i : 8 * i + 8, :] = tile
    between()
    lane = lax.broadcasted_iota(jnp.int32, (BLOCK, size), 1)
    top = top_ref[...]
    panel = dot(top, work[here, :])
    work[here, :] = jnp.where(lane < off, panel, 0.0)
    work[here, here] = top

    @pl.when(b + 1 < size // BLOCK)
    def _():
        after = jnp.where(lane >= off + BLOCK, panel, 0.0)
        shape = (size - BLOCK, size)
        below = lax.broadcasted_iota(jnp.int32, shape, 0) >= off
        lanes = lax.broadcasted_iota(jnp.int32, shape, 1)
        gone = below & (lanes >= off) & (lanes < off + BLOCK)
        row = work[here, :] + after
        work[BLOCK:, :] = jnp.where(gone, 0.0, work[BLOCK:, :]) - dot(after[:, BLOCK:], row, 0, 0)


def kernel(
    zs_n, ys_n, total_rows, ratio, m_ref, g_ref, q_ref, update_ref, momentum_ref, left_ref, basis_ref,
    part, ybuf, chunks, raw, gpart, gcbuf, gxsum, gxbuf, gzsum, gzbuf, gfull,
    wpart, wcbuf, wxsum, wxbuf, wzsum, wzbuf, wfull, work, top, right, norms,
    s_y, r_y, s_y2, r_y2, s_n, r_n,
    s_hc, r_hc, s_hx, r_hx, s_hz, r_hz, s_gy, r_gy, s_gx, r_gx, s_gc, r_gc,
    s_c, r_c, s_x, r_x, s_z, r_z, s_wz, r_wz, s_wx, r_wx, s_wc, r_wc,
):
    z, x, core, y = place()
    half = part.shape[1]
    lanes = part.shape[2]
    across = raw.shape[1] // lanes

    def send(src, dst, ssem, rsem, to):
        pltpu.make_async_remote_copy(
            src_ref=src, dst_ref=dst, send_sem=ssem, recv_sem=rsem, device_id=to, device_id_type=MESH
        ).start()

    def done(ref, sem):
        pltpu.make_async_copy(ref, ref, sem).wait()

    def total(ref):
        acc = ref[0]
        for k in range(1, ref.shape[0]):
            acc = acc + ref[k]
        return acc

    def x_of(d):
        return (x + d) % XS

    def y_of(d):
        return (y + d) % ys_n

    def z_of(d):
        return (z + d) % zs_n

    def at_x(k):
        return device(z, k, core, y)

    def at_y(k):
        return device(z, x, core, k)

    def at_z(k):
        return device(k, x, core, y)

    partner = device(z, x, 1 - core, y)
    barrier = pltpu.get_barrier_semaphore()

    def greet(to):
        pl.semaphore_signal(barrier, inc=1, device_id=to, device_id_type=MESH)

    each(1, ys_n, lambda d: greet(at_y(y_of(d))))
    greet(partner)
    each(1, XS, lambda d: greet(at_x(x_of(d))))
    each(1, zs_n, lambda d: greet(at_z(z_of(d))))

    summed = split(m_ref[...] + g_ref[...].astype(jnp.float32))
    left_part = dot3(summed, split(q_ref[...]))
    for k in range(ys_n):
        row, col = k // across, k % across
        part[k] = left_part[row * half : (row + 1) * half, col * lanes : (col + 1) * lanes]
    pl.semaphore_wait(barrier, (ys_n - 1) + 1 + (XS - 1) + (zs_n - 1))

    each(1, ys_n, lambda d: send(part.at[y_of(d)], ybuf.at[y], s_y.at[d], r_y.at[y], at_y(y_of(d))))
    ybuf[y] = part[y]
    each(1, ys_n, lambda d: done(ybuf.at[y_of(d)], r_y.at[y_of(d)]))
    chunks[y] = total(ybuf)
    each(1, ys_n, lambda d: send(chunks.at[y], chunks.at[y], s_y2.at[d], r_y2.at[y], at_y(y_of(d))))
    each(1, ys_n, lambda d: done(chunks.at[y_of(d)], r_y2.at[y_of(d)]))
    for k in range(ys_n):
        row, col = k // across, k % across
        raw[row * half : (row + 1) * half, col * lanes : (col + 1) * lanes] = chunks[k]

    per = gpart.shape[0]
    pair = raw[:, pl.ds(pl.multiple_of((y // per) * 128, 128), 128)]
    gpart[...] = dot(pair, raw[...], 0, 0).reshape(gpart.shape)
    plane = y % per
    ghalf = gpart.at[plane, :, 1 - core]
    send(ghalf, gcbuf, s_hc, r_hc, partner)

    wpart[...] = dot3(summed, split(raw[...]), 0, 0).reshape(wpart.shape)
    each(1, XS + 1, lambda d: send(
        wpart.at[:, x_of(d), 1 - core], wcbuf.at[x_of(d)], s_c.at[d - 1], r_c.at[x_of(d)], partner))

    done(gcbuf, r_hc)
    gxsum[...] = gpart[plane, :, core] + gcbuf[...]
    each(1, XS, lambda d: send(gxsum.at[x_of(d)], gxbuf.at[x], s_hx.at[d], r_hx.at[x], at_x(x_of(d))))
    gxbuf[x] = gxsum[x]

    def w_forward(d):
        k = x_of(d)
        done(wcbuf.at[k], r_c.at[k])
        wxsum[k] = wpart[:, k, core] + wcbuf[k]
        send(wxsum.at[k], wxbuf.at[x], s_x.at[d], r_x.at[x], at_x(k))

    each(1, XS, w_forward)
    each(1, XS, lambda d: done(gxbuf.at[x_of(d)], r_hx.at[x_of(d)]))
    gzsum[...] = total(gxbuf)
    each(1, zs_n, lambda d: send(gzsum, gzbuf.at[z], s_hz.at[d], r_hz.at[z], at_z(z_of(d))))
    gzbuf[z] = gzsum[...]
    done(wcbuf.at[x], r_c.at[x])
    wxbuf[x] = wpart[:, x, core] + wcbuf[x]

    each(1, zs_n, lambda d: done(gzbuf.at[z_of(d)], r_hz.at[z_of(d)]))
    gfull[y, x, core] = total(gzbuf)
    gown = gfull.at[y, x, core]
    each(1, ys_n, lambda d: send(gown, gown, s_gy.at[d], r_gy.at[y], at_y(y_of(d))))

    each(1, XS, lambda d: done(wxbuf.at[x_of(d)], r_x.at[x_of(d)]))
    wzsum[...] = total(wxbuf)
    each(1, zs_n, lambda d: send(wzsum.at[z_of(d)], wzbuf.at[z], s_z.at[d], r_z.at[z], at_z(z_of(d))))
    wzbuf[z] = wzsum[z]

    each(1, ys_n, lambda d: done(gfull.at[y_of(d), x, core], r_gy.at[y_of(d)]))
    gx = gfull.at[:, x, core]
    each(1, XS, lambda d: send(gx, gx, s_gx.at[d], r_gx.at[x], at_x(x_of(d))))
    each(1, XS, lambda d: done(gfull.at[:, x_of(d), core], r_gx.at[x_of(d)]))
    gc = gfull.at[:, :, core]
    send(gc, gc, s_gc, r_gc, partner)
    done(gfull.at[:, :, 1 - core], r_gc)
    work[...] = gfull[...].reshape(work.shape)

    each(1, zs_n, lambda d: done(wzbuf.at[z_of(d)], r_z.at[z_of(d)]))
    wfull[z, x, core] = total(wzbuf)
    wown = wfull.at[z, x, core]
    each(1, zs_n, lambda d: send(wown, wown, s_wz.at[d], r_wz.at[z], at_z(z_of(d))))
    wx = wfull.at[:, x, core]
    wc = wfull.at[:, :, core]

    @pl.loop(0, work.shape[0] // BLOCK)
    def _(b):
        def between():
            @pl.when(b == 0)
            def _():
                each(1, zs_n, lambda d: done(wfull.at[z_of(d), x, core], r_wz.at[z_of(d)]))
                each(1, XS, lambda d: send(wx, wx, s_wx.at[d], r_wx.at[x], at_x(x_of(d))))

            @pl.when(b == 2)
            def _():
                each(1, XS, lambda d: done(wfull.at[:, x_of(d), core], r_wx.at[x_of(d)]))
                send(wc, wc, s_wc, r_wc, partner)

        factor_step(b, work, top, between)

    done(wfull.at[:, :, 1 - core], r_wc)

    inverse = split(work[...])
    right[...] = dot3(split(wfull[...].reshape(right.shape)), inverse, 1, 1)
    values = right[...]
    norms[y] = jnp.sum(values * values, axis=0, keepdims=True)
    each(1, ys_n, lambda d: send(norms.at[y], norms.at[y], s_n.at[d], r_n.at[y], at_y(y_of(d))))
    rows = split(values)
    left = dot3(split(raw[...]), inverse, 1, 1)
    left_ref[...] = left * math.sqrt(total_rows)
    product = dot3(split(left), rows, 1, 1)
    momentum_ref[...] = (m_ref[...] + g_ref[...].astype(jnp.float32)) - 0.5 * product
    each(1, ys_n, lambda d: done(norms.at[y_of(d)], r_n.at[y_of(d)]))
    column_norm = jnp.sqrt(total(norms) + EPSILON)
    update_ref[...] = dot3(split(left * (ratio / column_norm)), rows, 1, 1).astype(update_ref.dtype)
    me = pl.multiple_of(lax.axis_index("fsdp") * 8, 8)
    basis_ref[...] = right[pl.ds(me, 8), :] / column_norm

    def sent_y(d):
        done(part.at[y_of(d)], s_y.at[d])
        done(chunks.at[y], s_y2.at[d])
        done(gown, s_gy.at[d])
        done(norms.at[y], s_n.at[d])

    def sent_x(d):
        done(gxsum.at[x_of(d)], s_hx.at[d])
        done(gx, s_gx.at[d])
        done(wxsum.at[x_of(d)], s_x.at[d])
        done(wx, s_wx.at[d])

    def sent_z(d):
        done(gzsum, s_hz.at[d])
        done(wzsum.at[z_of(d)], s_z.at[d])
        done(wown, s_wz.at[d])

    each(1, ys_n, sent_y)
    each(1, XS, sent_x)
    each(1, zs_n, sent_z)
    each(1, XS + 1, lambda d: done(wpart.at[:, x_of(d), 1 - core], s_c.at[d - 1]))
    done(ghalf, s_hc)
    done(gc, s_gc)
    done(wc, s_wc)


def on_device(momentum, gradient, right_basis):
    rows, cols = momentum.shape
    rank = right_basis.shape[1]
    groups = lax.axis_size("fsdp")
    ys_n = lax.axis_size("tensor")
    zs_n = groups // (XS * CORES)
    total_rows = rows * groups
    ratio = math.sqrt(total_rows / (cols * ys_n))
    f32 = jnp.float32
    lanes = 128
    half = rows * rank // (ys_n * lanes)
    per = lanes * ys_n // rank

    def buffer(*shape):
        return pltpu.VMEM(shape, f32)

    one = [pltpu.SemaphoreType.DMA] * 2

    def sems(n):
        return [pltpu.SemaphoreType.DMA((n,))] * 2

    gsum = buffer(XS, 8, rank)
    wsum = buffer(XS, zs_n, 8, rank)
    vmem = pl.BlockSpec(memory_space=pltpu.VMEM)
    return pl.pallas_call(
        functools.partial(kernel, zs_n, ys_n, total_rows, ratio),
        name="step",
        out_shape=(
            jax.ShapeDtypeStruct((rows, cols), jnp.bfloat16),
            jax.ShapeDtypeStruct((rows, cols), f32),
            jax.ShapeDtypeStruct((rows, rank), f32),
            jax.ShapeDtypeStruct((8, rank), f32),
        ),
        in_specs=[vmem] * 3,
        out_specs=(vmem,) * 4,
        scratch_shapes=[
            buffer(ys_n, half, lanes), buffer(ys_n, half, lanes), buffer(ys_n, half, lanes), buffer(rows, rank),
            buffer(per, XS, CORES, 8, rank), gsum, gsum, gsum, buffer(8, rank), buffer(zs_n, 8, rank),
            buffer(ys_n, XS, CORES, 8, rank),
            buffer(zs_n, XS, CORES, 8, rank), wsum, wsum, wsum, buffer(zs_n, 8, rank), buffer(zs_n, 8, rank),
            buffer(zs_n, XS, CORES, 8, rank),
            buffer(rank, rank), buffer(BLOCK, BLOCK), buffer(cols, rank), buffer(ys_n, 1, rank),
            *sems(ys_n), *sems(ys_n), *sems(ys_n),
            *one, *sems(XS), *sems(zs_n), *sems(ys_n), *sems(XS), *one,
            *sems(XS), *sems(XS), *sems(zs_n), *sems(zs_n), *sems(XS), *one,
        ],
        compiler_params=pltpu.CompilerParams(
            collective_id=0, has_side_effects=True, vmem_limit_bytes=VMEM_LIMIT
        ),
    )(momentum, gradient, right_basis)


def solution(mesh):
    in_specs = (P("fsdp", "tensor"), P("fsdp", "tensor"), P("tensor", None))
    out_specs = (
        P("fsdp", "tensor"),
        P("fsdp", "tensor"),
        P("fsdp", None),
        P(("tensor", "fsdp"), None),
    )
    return jax.shard_map(
        on_device, mesh=mesh, in_specs=in_specs, out_specs=out_specs, check_vma=False
    )
```

```python
import functools
import math

import jax
import jax.numpy as jnp
from jax import lax
from jax.experimental import pallas as pl
from jax.experimental.pallas import tpu as pltpu
from jax.sharding import PartitionSpec as P

EPSILON = 1e-06
HIGHEST = lax.Precision.HIGHEST
MESH = pl.DeviceIdType.MESH
XS, CORES = 4, 2
VMEM_LIMIT = 24 * 1024 * 1024


def dot(a, b, lhs=1, rhs=0):
    return lax.dot_general(
        a, b, (((lhs,), (rhs,)), ((), ())), precision=HIGHEST, preferred_element_type=jnp.float32
    )


def split(a):
    high = a.astype(jnp.bfloat16)
    return high, (a - high.astype(jnp.float32)).astype(jnp.bfloat16)


def dot3(a, b, lhs=1, rhs=0):
    def one(p, q):
        return lax.dot_general(p, q, (((lhs,), (rhs,)), ((), ())), preferred_element_type=jnp.float32)

    return one(a[0], b[0]) + (one(a[0], b[1]) + one(a[1], b[0]))


def place():
    f = lax.axis_index("fsdp")
    y = lax.axis_index("tensor")
    return f // (XS * CORES), (f // CORES) % XS, f % CORES, y


def device(z, x, core, y):
    return ((z * XS + x) * CORES + core, y)


def each(start, stop, body):
    def step(i, carry):
        body(i)
        return carry

    lax.fori_loop(start, stop, step, 0)


def each_peer(count, body):
    def step(k):
        off = (k + 1) // 2
        body(count // 2 + off * (1 - 2 * (k % 2)))

    each(0, count - 1, step)


BLOCK = 128


def factor_block(tiles):
    shape = (8, BLOCK)
    lane = lax.broadcasted_iota(jnp.int32, shape, 1)
    sub = lax.broadcasted_iota(jnp.int32, shape, 0)
    count = len(tiles)
    out = []

    def column(tile, k):
        return jnp.broadcast_to(tile[:, k : k + 1], shape)

    def row(tile, k):
        return jnp.broadcast_to(tile[k : k + 1, :], shape)

    tiles = list(tiles)
    for t in range(count):
        base = 8 * t
        here = (lane >= base) & (lane < base + 8)
        tile = tiles[t]
        cols = [column(tile, base + c) for c in range(8)]
        start = jnp.where(here, jnp.where(lane - base == sub, 1.0, 0.0), tile)
        scale, rows, low = [], [], {}
        for p in range(8):
            r = row(lax.rsqrt(cols[p]), p)
            lp = cols[p] * r
            for c in range(p + 1, 8):
                low[p, c] = row(lp, c)
                cols[c] = cols[c] - lp * low[p, c]
            w = row(start, p)
            for q in range(p):
                w = w - low[q, p] * rows[q]
            rows.append(w * r)
            scale.append(r)
        done = rows[7]
        for p in range(7):
            done = jnp.where(sub == p, rows[p], done)
        out.append(jnp.where(lane < base + 8, done, 0.0))
        if t + 1 == count:
            break
        solved = [None] * 8
        for p in reversed(range(8)):
            w = rows[p]
            for q in reversed(range(p + 1, 8)):
                w = w - low[p, q] * solved[q]
            solved[p] = w * scale[p]
        for i in range(t + 1, count):
            acc = jnp.where(here, 0.0, tiles[i])
            for p in reversed(range(8)):
                acc = acc - column(tiles[i], base + p) * solved[p]
            tiles[i] = acc
    return out


def factor_step(b, work, top_ref, between):
    size = work.shape[0]
    off = pl.multiple_of(b * BLOCK, BLOCK)
    here = pl.ds(off, BLOCK)
    tiles = [work[pl.ds(pl.multiple_of(off + 8 * i, 8), 8), here] for i in range(BLOCK // 8)]
    for i, tile in enumerate(factor_block(tiles)):
        top_ref[8 * i : 8 * i + 8, :] = tile
    between()
    lane = lax.broadcasted_iota(jnp.int32, (BLOCK, size), 1)
    top = top_ref[...]
    inverse = split(top)
    panel = dot3(inverse, split(work[here, :]))
    work[here, :] = jnp.where(lane < off, panel, 0.0)
    work[here, here] = top

    @pl.when(b + 1 < size // BLOCK)
    def _():
        after = jnp.where(lane >= off + BLOCK, panel, 0.0)
        shape = (size - BLOCK, size)
        below = lax.broadcasted_iota(jnp.int32, shape, 0) >= off
        lanes = lax.broadcasted_iota(jnp.int32, shape, 1)
        gone = below & (lanes >= off) & (lanes < off + BLOCK)
        row = work[here, :] + after
        work[BLOCK:, :] = jnp.where(gone, 0.0, work[BLOCK:, :]) - dot3(split(after[:, BLOCK:]), split(row), 0, 0)


def kernel(
    zs_n, ys_n, total_rows, ratio, m_ref, g_ref, q_ref, update_ref, momentum_ref, left_ref, basis_ref,
    part, ybuf, ysum, chunks, raw, gpart, gcbuf, gxsum, gxbuf, gzsum, gzbuf, gfull,
    wpart, wcbuf, wxsum, wxbuf, wzsum, wzbuf, wfull, work, top, right, norms,
    s_y, r_y, s_y2, r_y2, s_n, r_n,
    s_hc, r_hc, s_hx, r_hx, s_hz, r_hz, s_gy, r_gy, s_gx, r_gx, s_gc, r_gc,
    s_c, r_c, s_x, r_x, s_z, r_z, s_wz, r_wz, s_wx, r_wx, s_wc, r_wc,
):
    z, x, core, y = place()
    half = part.shape[1]
    lanes = part.shape[2]
    rank = raw.shape[1]
    across = rank // lanes

    def send(src, dst, ssem, rsem, to):
        pltpu.make_async_remote_copy(
            src_ref=src, dst_ref=dst, send_sem=ssem, recv_sem=rsem, device_id=to, device_id_type=MESH
        ).start()

    def done(ref, sem):
        pltpu.make_async_copy(ref, ref, sem).wait()

    def total(ref):
        acc = ref[0]
        for k in range(1, ref.shape[0]):
            acc = acc + ref[k]
        return acc

    def x_of(d):
        return (x + d) % XS

    def y_of(d):
        return (y + d) % ys_n

    def z_of(d):
        return (z + d) % zs_n

    def at_x(k):
        return device(z, k, core, y)

    def at_y(k):
        return device(z, x, core, k)

    def at_z(k):
        return device(k, x, core, y)

    partner = device(z, x, 1 - core, y)
    barrier = pltpu.get_barrier_semaphore()

    def greet(to):
        pl.semaphore_signal(barrier, inc=1, device_id=to, device_id_type=MESH)

    each(1, ys_n, lambda d: greet(at_y(y_of(d))))
    greet(partner)
    each(1, XS, lambda d: greet(at_x(x_of(d))))
    each(1, zs_n, lambda d: greet(at_z(z_of(d))))

    summed = split(m_ref[...] + g_ref[...].astype(jnp.float32))
    left_part = dot3(summed, split(q_ref[...]))
    for k in range(ys_n):
        row, col = k // across, k % across
        part[k] = left_part[row * half : (row + 1) * half, col * lanes : (col + 1) * lanes]
    pl.semaphore_wait(barrier, (ys_n - 1) + 1 + (XS - 1) + (zs_n - 1))

    ways = ((1, ys_n // 2), (-1, (ys_n - 1) // 2))
    most = ways[0][1]
    cut = half // 16 * 8 + 8
    pieces = (slice(0, cut), slice(cut, half))

    def slot(way, step):
        return way * most + step - 1

    def sem(way, step, piece):
        return slot(way, step) * len(pieces) + piece

    def hops():
        for step in range(1, most + 1):
            for piece, rows in enumerate(pieces):
                for way, (sign, steps) in enumerate(ways):
                    if step <= steps:
                        yield step, piece, rows, way, sign, steps

    for step, piece, rows, way, sign, steps in hops():
        to = (y + sign * (steps + 1 - step) + ys_n) % ys_n
        out = part.at[to, rows]
        if step > 1:
            came = slot(way, step - 1)
            done(ybuf.at[came, rows], r_y.at[sem(way, step - 1, piece)])
            ysum[came + 1, rows] = ybuf[came, rows] + part[to, rows]
            out = ysum.at[came + 1, rows]
        k = sem(way, step, piece)
        send(out, ybuf.at[slot(way, step), rows], s_y.at[k], r_y.at[k], at_y((y + sign + ys_n) % ys_n))
    for piece, rows in enumerate(pieces):
        acc = part[y, rows]
        for way, (sign, steps) in enumerate(ways):
            done(ybuf.at[slot(way, steps), rows], r_y.at[sem(way, steps, piece)])
            acc = acc + ybuf[slot(way, steps), rows]
        chunks[y, rows] = acc
    for step, piece, rows, way, sign, steps in hops():
        block = chunks.at[(y - sign * (step - 1) + ys_n) % ys_n, rows]
        if step > 1:
            done(block, r_y2.at[sem(way, step - 1, piece)])
        k = sem(way, step, piece)
        send(block, block, s_y2.at[k], r_y2.at[k], at_y((y + sign + ys_n) % ys_n))
    for piece, rows in enumerate(pieces):
        for way, (sign, steps) in enumerate(ways):
            done(chunks.at[(y - sign * steps + ys_n) % ys_n, rows], r_y2.at[sem(way, steps, piece)])
    for k in range(ys_n):
        row, col = k // across, k % across
        raw[row * half : (row + 1) * half, col * lanes : (col + 1) * lanes] = chunks[k]

    per = gpart.shape[0]
    pair = raw[:, pl.ds(pl.multiple_of((y // per) * 128, 128), 128)]
    gpart[...] = dot(pair, raw[...], 0, 0).reshape(gpart.shape)
    plane = y % per
    ghalf = gpart.at[plane, :, 1 - core]
    send(ghalf, gcbuf, s_hc, r_hc, partner)

    wpart[...] = dot3(summed, split(raw[...]), 0, 0).reshape(wpart.shape)

    def w_across(d):
        send(wpart.at[:, x_of(d), 1 - core], wcbuf.at[x_of(d)], s_c.at[d], r_c.at[x_of(d)], partner)

    each_peer(XS, w_across)
    w_across(0)

    done(gcbuf, r_hc)
    gxsum[...] = gpart[plane, :, core] + gcbuf[...]
    each_peer(XS, lambda d: send(gxsum.at[x_of(d)], gxbuf.at[x], s_hx.at[d], r_hx.at[x], at_x(x_of(d))))
    gxbuf[x] = gxsum[x]

    def w_forward(d):
        k = x_of(d)
        done(wcbuf.at[k], r_c.at[k])
        wxsum[k] = wpart[:, k, core] + wcbuf[k]
        send(wxsum.at[k], wxbuf.at[x], s_x.at[d], r_x.at[x], at_x(k))

    each_peer(XS, w_forward)
    each(1, XS, lambda d: done(gxbuf.at[x_of(d)], r_hx.at[x_of(d)]))
    gzsum[...] = total(gxbuf)
    each_peer(zs_n, lambda d: send(gzsum, gzbuf.at[z], s_hz.at[d], r_hz.at[z], at_z(z_of(d))))
    gzbuf[z] = gzsum[...]
    done(wcbuf.at[x], r_c.at[x])
    wxbuf[x] = wpart[:, x, core] + wcbuf[x]

    each(1, zs_n, lambda d: done(gzbuf.at[z_of(d)], r_hz.at[z_of(d)]))
    gfull[y, x, core] = total(gzbuf)
    gown = gfull.at[y, x, core]
    each_peer(ys_n, lambda d: send(gown, gown, s_gy.at[d], r_gy.at[y], at_y(y_of(d))))

    each(1, XS, lambda d: done(wxbuf.at[x_of(d)], r_x.at[x_of(d)]))
    wzsum[...] = total(wxbuf)
    each_peer(zs_n, lambda d: send(wzsum.at[z_of(d)], wzbuf.at[z], s_z.at[d], r_z.at[z], at_z(z_of(d))))
    wzbuf[z] = wzsum[z]

    each(1, ys_n, lambda d: done(gfull.at[y_of(d), x, core], r_gy.at[y_of(d)]))
    blocks = range(rank // lanes)

    def upper(block, *at):
        return gfull.at[(slice(0, per * (block + 1)), *at, slice(None), slice(block * lanes, (block + 1) * lanes))]

    def gather_x(d):
        for k in blocks:
            mine = upper(k, x, core)
            send(mine, mine, s_gx.at[d * len(blocks) + k], r_gx.at[x * len(blocks) + k], at_x(x_of(d)))

    def gathered_x(d):
        for k in blocks:
            done(upper(k, x_of(d), core), r_gx.at[x_of(d) * len(blocks) + k])

    each_peer(XS, gather_x)
    each(1, XS, gathered_x)
    for k in blocks:
        send(upper(k, slice(None), core), upper(k, slice(None), core), s_gc.at[k], r_gc.at[k], partner)
    for k in blocks:
        done(upper(k, slice(None), 1 - core), r_gc.at[k])
        end = (k + 1) * lanes
        here = slice(k * lanes, end)
        work[0:end, here] = gfull[0 : per * (k + 1), :, :, :, here].reshape(end, lanes)
        if end < rank:
            work[end:, here] = jnp.zeros((rank - end, lanes), jnp.float32)

    each(1, zs_n, lambda d: done(wzbuf.at[z_of(d)], r_z.at[z_of(d)]))
    wfull[z, x, core] = total(wzbuf)
    wown = wfull.at[z, x, core]
    each_peer(zs_n, lambda d: send(wown, wown, s_wz.at[d], r_wz.at[z], at_z(z_of(d))))
    wx = wfull.at[:, x, core]
    wc = wfull.at[:, :, core]

    @pl.loop(0, work.shape[0] // BLOCK)
    def _(b):
        def between():
            @pl.when(b == 0)
            def _():
                each(1, zs_n, lambda d: done(wfull.at[z_of(d), x, core], r_wz.at[z_of(d)]))
                each_peer(XS, lambda d: send(wx, wx, s_wx.at[d], r_wx.at[x], at_x(x_of(d))))

            @pl.when(b == 2)
            def _():
                each(1, XS, lambda d: done(wfull.at[:, x_of(d), core], r_wx.at[x_of(d)]))
                send(wc, wc, s_wc, r_wc, partner)

        factor_step(b, work, top, between)

    done(wfull.at[:, :, 1 - core], r_wc)

    inverse = split(work[...])
    right[...] = dot3(split(wfull[...].reshape(right.shape)), inverse, 1, 1)
    values = right[...]
    norms[y] = jnp.sum(values * values, axis=0, keepdims=True)
    each_peer(ys_n, lambda d: send(norms.at[y], norms.at[y], s_n.at[d], r_n.at[y], at_y(y_of(d))))
    right_parts = split(values)
    left = dot3(split(raw[...]), inverse, 1, 1)
    left_ref[...] = left * math.sqrt(total_rows)
    product = dot3(split(left), right_parts, 1, 1)
    momentum_ref[...] = (m_ref[...] + g_ref[...].astype(jnp.float32)) - 0.5 * product
    each(1, ys_n, lambda d: done(norms.at[y_of(d)], r_n.at[y_of(d)]))
    column_norm = jnp.sqrt(total(norms) + EPSILON)
    update_ref[...] = dot3(split(left * (ratio / column_norm)), right_parts, 1, 1).astype(update_ref.dtype)
    me = pl.multiple_of(lax.axis_index("fsdp") * 8, 8)
    basis_ref[...] = right[pl.ds(me, 8), :] / column_norm

    def sent_y(d):
        done(gown, s_gy.at[d])
        done(norms.at[y], s_n.at[d])

    def sent_x(d):
        done(gxsum.at[x_of(d)], s_hx.at[d])
        for k in blocks:
            done(upper(k, x, core), s_gx.at[d * len(blocks) + k])
        done(wxsum.at[x_of(d)], s_x.at[d])
        done(wx, s_wx.at[d])

    def sent_z(d):
        done(gzsum, s_hz.at[d])
        done(wzsum.at[z_of(d)], s_z.at[d])
        done(wown, s_wz.at[d])

    each(1, ys_n, sent_y)
    each(1, XS, sent_x)
    each(1, zs_n, sent_z)
    each(0, XS, lambda d: done(wpart.at[:, x_of(d), 1 - core], s_c.at[d]))
    done(ghalf, s_hc)
    for k in blocks:
        done(upper(k, slice(None), core), s_gc.at[k])
    for step, piece, rows, way, sign, steps in hops():
        k = sem(way, step, piece)
        done(part.at[y, rows], s_y.at[k])
        done(chunks.at[y, rows], s_y2.at[k])
    done(wc, s_wc)


def on_device(momentum, gradient, right_basis):
    rows, cols = momentum.shape
    rank = right_basis.shape[1]
    groups = lax.axis_size("fsdp")
    ys_n = lax.axis_size("tensor")
    zs_n = groups // (XS * CORES)
    total_rows = rows * groups
    ratio = math.sqrt(total_rows / (cols * ys_n))
    f32 = jnp.float32
    lanes = 128
    half = rows * rank // (ys_n * lanes)
    per = lanes * ys_n // rank

    def buffer(*shape):
        return pltpu.VMEM(shape, f32)

    one = [pltpu.SemaphoreType.DMA] * 2

    def sems(n):
        return [pltpu.SemaphoreType.DMA((n,))] * 2

    gsum = buffer(XS, 8, rank)
    wsum = buffer(XS, zs_n, 8, rank)
    vmem = pl.BlockSpec(memory_space=pltpu.VMEM)
    return pl.pallas_call(
        functools.partial(kernel, zs_n, ys_n, total_rows, ratio),
        name="step",
        out_shape=(
            jax.ShapeDtypeStruct((rows, cols), jnp.bfloat16),
            jax.ShapeDtypeStruct((rows, cols), f32),
            jax.ShapeDtypeStruct((rows, rank), f32),
            jax.ShapeDtypeStruct((8, rank), f32),
        ),
        in_specs=[vmem] * 3,
        out_specs=(vmem,) * 4,
        scratch_shapes=[
            buffer(ys_n, half, lanes), buffer(ys_n, half, lanes), buffer(ys_n, half, lanes), buffer(ys_n, half, lanes),
            buffer(rows, rank),
            buffer(per, XS, CORES, 8, rank), gsum, gsum, gsum, buffer(8, rank), buffer(zs_n, 8, rank),
            buffer(ys_n, XS, CORES, 8, rank),
            buffer(zs_n, XS, CORES, 8, rank), wsum, wsum, wsum, buffer(zs_n, 8, rank), buffer(zs_n, 8, rank),
            buffer(zs_n, XS, CORES, 8, rank),
            buffer(rank, rank), buffer(BLOCK, BLOCK), buffer(cols, rank), buffer(ys_n, 1, rank),
            *sems(2 * ys_n), *sems(2 * ys_n), *sems(ys_n),
            *one, *sems(XS), *sems(zs_n), *sems(ys_n), *sems(XS * rank // lanes), *sems(rank // lanes),
            *sems(XS), *sems(XS), *sems(zs_n), *sems(zs_n), *sems(XS), *one,
        ],
        compiler_params=pltpu.CompilerParams(
            collective_id=0, has_side_effects=True, vmem_limit_bytes=VMEM_LIMIT
        ),
    )(momentum, gradient, right_basis)


def solution(mesh):
    in_specs = (P("fsdp", "tensor"), P("fsdp", "tensor"), P("tensor", None))
    out_specs = (
        P("fsdp", "tensor"),
        P("fsdp", "tensor"),
        P("fsdp", None),
        P(("tensor", "fsdp"), None),
    )
    return jax.shard_map(
        on_device, mesh=mesh, in_specs=in_specs, out_specs=out_specs, check_vma=False
    )
```

```python
import functools
import math

import jax
import jax.numpy as jnp
from jax import lax
from jax.experimental import pallas as pl
from jax.experimental.pallas import tpu as pltpu
from jax.sharding import PartitionSpec as P

EPSILON = 1e-06
HIGHEST = lax.Precision.HIGHEST
MESH = pl.DeviceIdType.MESH
XS, CORES = 4, 2
VMEM_LIMIT = 24 * 1024 * 1024


def dot(a, b, lhs=1, rhs=0):
    return lax.dot_general(
        a, b, (((lhs,), (rhs,)), ((), ())), precision=HIGHEST, preferred_element_type=jnp.float32
    )


def split(a):
    high = a.astype(jnp.bfloat16)
    return high, (a - high.astype(jnp.float32)).astype(jnp.bfloat16)


def dot3(a, b, lhs=1, rhs=0):
    def one(p, q):
        return lax.dot_general(p, q, (((lhs,), (rhs,)), ((), ())), preferred_element_type=jnp.float32)

    return one(a[0], b[0]) + (one(a[0], b[1]) + one(a[1], b[0]))


def place():
    f = lax.axis_index("fsdp")
    y = lax.axis_index("tensor")
    return f // (XS * CORES), (f // CORES) % XS, f % CORES, y


def device(z, x, core, y):
    return ((z * XS + x) * CORES + core, y)


def each(start, stop, body):
    def step(i, carry):
        body(i)
        return carry

    lax.fori_loop(start, stop, step, 0)


def far_first(count):
    return sorted(range(1, count), key=lambda d: -min(d, count - d))


BLOCK = 128
GROUP, NEAR = 4, 1


def factor_block(tiles, panel_ref):
    shape = (8, BLOCK)
    lane = lax.broadcasted_iota(jnp.int32, shape, 1)
    sub = lax.broadcasted_iota(jnp.int32, shape, 0)
    count = len(tiles)
    out = []

    def column(tile, k):
        return jnp.broadcast_to(tile[:, k : k + 1], shape)

    def row(tile, k):
        return jnp.broadcast_to(tile[k : k + 1, :], shape)

    tiles = list(tiles)
    for t in range(count):
        base = 8 * t
        first = t // GROUP * GROUP
        end = first + GROUP
        near = min(end + NEAR, count)
        here = (lane >= base) & (lane < base + 8)
        tile = tiles[t]
        cols = [column(tile, base + c) for c in range(8)]
        start = jnp.where(here, jnp.where(lane - base == sub, 1.0, 0.0), tile)
        scale, rows, low = [], [], {}
        for p in range(8):
            r = row(lax.rsqrt(cols[p]), p)
            lp = cols[p] * r
            for c in range(p + 1, 8):
                low[p, c] = row(lp, c)
                cols[c] = cols[c] - lp * low[p, c]
            w = row(start, p)
            for q in range(p):
                w = w - low[q, p] * rows[q]
            rows.append(w * r)
            scale.append(r)
        done = rows[7]
        for p in range(7):
            done = jnp.where(sub == p, rows[p], done)
        out.append(jnp.where(lane < base + 8, done, 0.0))
        panel_ref[base - 8 * first : base - 8 * first + 8, :] = jnp.where((lane < base + 8) | (lane >= 8 * end), done, 0.0)
        if t + 1 == count:
            break
        solved = [None] * 8
        for p in reversed(range(8)):
            w = rows[p]
            for q in reversed(range(p + 1, 8)):
                w = w - low[p, q] * solved[q]
            solved[p] = w * scale[p]
        for i in range(t + 1, near):
            acc = jnp.where(here, 0.0, tiles[i])
            for p in reversed(range(8)):
                acc = acc - column(tiles[i], base + p) * solved[p]
            tiles[i] = acc
        if t + 1 == end and near < count:
            panel = panel_ref[...]
            low = jnp.where(lax.broadcasted_iota(jnp.int32, panel.shape, 1) >= 8 * near, panel, 0.0)
            change = dot3(split(low), split(panel), 0, 0)
            gone = (lane >= 8 * first) & (lane < 8 * end)
            for i in range(near, count):
                tiles[i] = jnp.where(gone, 0.0, tiles[i]) - change[8 * i : 8 * i + 8]
    return out


def factor_step(b, work, top_ref, panel_ref, between):
    size = work.shape[0]
    off = pl.multiple_of(b * BLOCK, BLOCK)
    here = pl.ds(off, BLOCK)
    tiles = [work[pl.ds(pl.multiple_of(off + 8 * i, 8), 8), here] for i in range(BLOCK // 8)]
    for i, tile in enumerate(factor_block(tiles, panel_ref)):
        top_ref[8 * i : 8 * i + 8, :] = tile
    between()
    lane = lax.broadcasted_iota(jnp.int32, (BLOCK, size), 1)
    top = top_ref[...]
    inverse = split(top)
    panel = dot3(inverse, split(work[here, :]))
    work[here, :] = jnp.where(lane < off, panel, 0.0)
    work[here, here] = top

    @pl.when(b + 1 < size // BLOCK)
    def _():
        after = jnp.where(lane >= off + BLOCK, panel, 0.0)
        shape = (size - BLOCK, size)
        below = lax.broadcasted_iota(jnp.int32, shape, 0) >= off
        lanes = lax.broadcasted_iota(jnp.int32, shape, 1)
        gone = below & (lanes >= off) & (lanes < off + BLOCK)
        row = work[here, :] + after
        work[BLOCK:, :] = jnp.where(gone, 0.0, work[BLOCK:, :]) - dot3(split(after[:, BLOCK:]), split(row), 0, 0)


def kernel(
    zs_n, ys_n, total_rows, ratio, m_hbm, g_hbm, q_hbm, update_ref, momentum_ref, left_ref, basis_ref,
    m_ref, g_ref, q_ref, s_in, part, ybuf, ysum, chunks, raw, gpart, gcbuf, gxsum, gxbuf, gzsum, gzbuf, gfull,
    wpart, wcbuf, wxsum, wxbuf, wzsum, wzbuf, wfull, work, top, panel, right, norms,
    s_y, r_y, s_y2, r_y2, s_n, r_n,
    s_hc, r_hc, s_hx, r_hx, s_hz, r_hz, s_gy, r_gy, s_gx, r_gx, s_gc, r_gc,
    s_c, r_c, s_x, r_x, s_z, r_z, s_wz, r_wz, s_wx, r_wx, s_wc, r_wc,
):
    loads = [
        pltpu.make_async_copy(src, dst, s_in.at[k])
        for k, (src, dst) in enumerate(((q_hbm, q_ref), (m_hbm, m_ref), (g_hbm, g_ref)))
    ]
    for load in loads:
        load.start()
    z, x, core, y = place()
    half = part.shape[1]
    lanes = part.shape[2]
    rank = raw.shape[1]
    across = rank // lanes

    def send(src, dst, ssem, rsem, to):
        pltpu.make_async_remote_copy(
            src_ref=src, dst_ref=dst, send_sem=ssem, recv_sem=rsem, device_id=to, device_id_type=MESH
        ).start()

    def done(ref, sem):
        pltpu.make_async_copy(ref, ref, sem).wait()

    def total(ref):
        acc = ref[0]
        for k in range(1, ref.shape[0]):
            acc = acc + ref[k]
        return acc

    def ring(at, count):
        known = [at] + [lax.rem(at + d, count) for d in range(1, count)]
        return lambda d: known[d] if isinstance(d, int) else lax.rem(at + d, count)

    x_of, y_of, z_of = ring(x, XS), ring(y, ys_n), ring(z, zs_n)

    def at_x(k):
        return device(z, k, core, y)

    def at_y(k):
        return device(z, x, core, k)

    def at_z(k):
        return device(k, x, core, y)

    partner = device(z, x, 1 - core, y)
    barrier = pltpu.get_barrier_semaphore()

    def greet(to):
        pl.semaphore_signal(barrier, inc=1, device_id=to, device_id_type=MESH)

    each(1, ys_n, lambda d: greet(at_y(y_of(d))))
    greet(partner)
    each(1, XS, lambda d: greet(at_x(x_of(d))))
    each(1, zs_n, lambda d: greet(at_z(z_of(d))))

    for load in loads:
        load.wait()
    m_ref[...] = m_ref[...] + g_ref[...].astype(jnp.float32)
    summed = split(m_ref[...])
    left_part = dot3(summed, split(q_ref[...]))
    for k in range(ys_n):
        row, col = k // across, k % across
        part[k] = left_part[row * half : (row + 1) * half, col * lanes : (col + 1) * lanes]
    pl.semaphore_wait(barrier, (ys_n - 1) + 1 + (XS - 1) + (zs_n - 1))

    ways = ((1, ys_n // 2), (-1, (ys_n - 1) // 2))
    most = ways[0][1]
    cut = half // 16 * 8 + 8
    pieces = (slice(0, cut), slice(cut, half))

    def slot(way, step):
        return way * most + step - 1

    def sem(way, step, piece):
        return slot(way, step) * len(pieces) + piece

    def hops():
        for step in range(1, most + 1):
            for piece, rows in enumerate(pieces):
                for way, (sign, steps) in enumerate(ways):
                    if step <= steps:
                        yield step, piece, rows, way, sign * (1 - 2 * piece), steps

    for step, piece, rows, way, sign, steps in hops():
        to = y_of((sign * (steps + 1 - step)) % ys_n)
        out = part.at[to, rows]
        if step > 1:
            came = slot(way, step - 1)
            done(ybuf.at[came, rows], r_y.at[sem(way, step - 1, piece)])
            ysum[came + 1, rows] = ybuf[came, rows] + part[to, rows]
            out = ysum.at[came + 1, rows]
        k = sem(way, step, piece)
        send(out, ybuf.at[slot(way, step), rows], s_y.at[k], r_y.at[k], at_y(y_of(sign % ys_n)))
    for piece, rows in enumerate(pieces):
        acc = part[y, rows]
        for way, (sign, steps) in enumerate(ways):
            done(ybuf.at[slot(way, steps), rows], r_y.at[sem(way, steps, piece)])
            acc = acc + ybuf[slot(way, steps), rows]
        chunks[y, rows] = acc
    for step, piece, rows, way, sign, steps in hops():
        block = chunks.at[y_of((-sign * (step - 1)) % ys_n), rows]
        if step > 1:
            done(block, r_y2.at[sem(way, step - 1, piece)])
        k = sem(way, step, piece)
        send(block, block, s_y2.at[k], r_y2.at[k], at_y(y_of(sign % ys_n)))
    for piece, rows in enumerate(pieces):
        for way, (sign, steps) in enumerate(ways):
            done(chunks.at[y_of((-sign * (1 - 2 * piece) * steps) % ys_n), rows], r_y2.at[sem(way, steps, piece)])
    for k in range(ys_n):
        row, col = k // across, k % across
        raw[row * half : (row + 1) * half, col * lanes : (col + 1) * lanes] = chunks[k]

    per = gpart.shape[0]
    pair = raw[:, pl.ds(pl.multiple_of((y // per) * 128, 128), 128)]
    gpart[...] = dot(pair, raw[...], 0, 0).reshape(gpart.shape)
    plane = y % per
    ghalf = gpart.at[plane, :, 1 - core]
    send(ghalf, gcbuf, s_hc, r_hc, partner)

    wpart[...] = dot3(summed, split(raw[...]), 0, 0).reshape(wpart.shape)

    def w_across(d):
        send(wpart.at[:, x_of(d), 1 - core], wcbuf.at[x_of(d)], s_c.at[d], r_c.at[x_of(d)], partner)

    for d in far_first(XS):
        w_across(d)
    w_across(0)

    done(gcbuf, r_hc)
    gxsum[...] = gpart[plane, :, core] + gcbuf[...]
    for d in far_first(XS):
        send(gxsum.at[x_of(d)], gxbuf.at[x], s_hx.at[d], r_hx.at[x], at_x(x_of(d)))
    gxbuf[x] = gxsum[x]

    def w_forward(d):
        k = x_of(d)
        done(wcbuf.at[k], r_c.at[k])
        wxsum[k] = wpart[:, k, core] + wcbuf[k]
        send(wxsum.at[k], wxbuf.at[x], s_x.at[d], r_x.at[x], at_x(k))

    for d in far_first(XS):
        w_forward(d)
    for d in range(1, XS):
        done(gxbuf.at[x_of(d)], r_hx.at[x_of(d)])
    gzsum[...] = total(gxbuf)
    for d in far_first(zs_n):
        send(gzsum, gzbuf.at[z], s_hz.at[d], r_hz.at[z], at_z(z_of(d)))
    gzbuf[z] = gzsum[...]
    done(wcbuf.at[x], r_c.at[x])
    wxbuf[x] = wpart[:, x, core] + wcbuf[x]

    for d in range(1, zs_n):
        done(gzbuf.at[z_of(d)], r_hz.at[z_of(d)])
    gfull[y, x, core] = total(gzbuf)
    gown = gfull.at[y, x, core]
    for d in far_first(ys_n):
        send(gown, gown, s_gy.at[d], r_gy.at[y], at_y(y_of(d)))

    for d in range(1, XS):
        done(wxbuf.at[x_of(d)], r_x.at[x_of(d)])
    wzsum[...] = total(wxbuf)
    for d in far_first(zs_n):
        send(wzsum.at[z_of(d)], wzbuf.at[z], s_z.at[d], r_z.at[z], at_z(z_of(d)))
    wzbuf[z] = wzsum[z]

    for d in range(1, ys_n):
        done(gfull.at[y_of(d), x, core], r_gy.at[y_of(d)])
    blocks = range(rank // lanes)

    def upper(block, *at):
        return gfull.at[(slice(0, per * (block + 1)), *at, slice(None), slice(block * lanes, (block + 1) * lanes))]

    def gather_x(d):
        for k in blocks:
            mine = upper(k, x, core)
            send(mine, mine, s_gx.at[d * len(blocks) + k], r_gx.at[x * len(blocks) + k], at_x(x_of(d)))

    def gathered_x(d):
        for k in blocks:
            done(upper(k, x_of(d), core), r_gx.at[x_of(d) * len(blocks) + k])

    for d in far_first(XS):
        gather_x(d)
    for d in range(1, XS):
        gathered_x(d)
    for k in blocks:
        send(upper(k, slice(None), core), upper(k, slice(None), core), s_gc.at[k], r_gc.at[k], partner)
    for d in range(1, zs_n):
        done(wzbuf.at[z_of(d)], r_z.at[z_of(d)])
    wfull[z, x, core] = total(wzbuf)
    wown = wfull.at[z, x, core]
    for d in far_first(zs_n):
        send(wown, wown, s_wz.at[d], r_wz.at[z], at_z(z_of(d)))
    for k in blocks:
        done(upper(k, slice(None), 1 - core), r_gc.at[k])
        end = (k + 1) * lanes
        here = slice(k * lanes, end)
        work[0:end, here] = gfull[0 : per * (k + 1), :, :, :, here].reshape(end, lanes)
        if end < rank:
            work[end:, here] = jnp.zeros((rank - end, lanes), jnp.float32)

    cutz = zs_n // 2
    halves = (slice(0, cutz), slice(cutz, zs_n))

    def w_at(k, zs=slice(None)):
        return wfull.at[zs, k, core]

    def w_core(k):
        send(w_at(k), w_at(k), s_wc.at[k], r_wc.at[k], partner)

    def w_start():
        for d in range(1, zs_n):
            done(wfull.at[z_of(d), x, core], r_wz.at[z_of(d)])
        send(w_at(x), w_at(x), s_wx.at[0], r_wx.at[0], at_x(x_of(1)))
        send(w_at(x), w_at(x), s_wx.at[1], r_wx.at[1], at_x(x_of(XS - 1)))
        w_core(x)

    def w_relay():
        behind, ahead = w_at(x_of(XS - 1), halves[0]), w_at(x_of(1), halves[1])
        done(w_at(x_of(XS - 1)), r_wx.at[0])
        send(behind, behind, s_wx.at[2], r_wx.at[2], at_x(x_of(1)))
        done(w_at(x_of(1)), r_wx.at[1])
        send(ahead, ahead, s_wx.at[3], r_wx.at[3], at_x(x_of(XS - 1)))
        w_core(x_of(1))
        w_core(x_of(XS - 1))

    @pl.loop(0, work.shape[0] // BLOCK)
    def _(b):
        def between():
            pl.when(b == 1)(w_start)
            pl.when(b == 2)(w_relay)

        factor_step(b, work, top, panel, between)

    for k, zs in enumerate(halves):
        done(w_at(x_of(2), zs), r_wx.at[2 + k])
    w_core(x_of(2))

    inverse = split(work[...])
    left = dot3(split(raw[...]), inverse, 1, 1)
    left_ref[...] = left * math.sqrt(total_rows)
    for d in range(XS):
        done(wfull.at[:, x_of(d), 1 - core], r_wc.at[x_of(d)])
    right[...] = dot3(split(wfull[...].reshape(right.shape)), inverse, 1, 1)
    values = right[...]
    norms[y] = jnp.sum(values * values, axis=0, keepdims=True)
    for d in far_first(ys_n):
        send(norms.at[y], norms.at[y], s_n.at[d], r_n.at[y], at_y(y_of(d)))
    right_parts = split(values)
    product = dot3(split(left), right_parts, 1, 1)
    momentum_ref[...] = m_ref[...] - 0.5 * product
    for d in range(1, ys_n):
        done(norms.at[y_of(d)], r_n.at[y_of(d)])
    column_norm = jnp.sqrt(total(norms) + EPSILON)
    update_ref[...] = dot3(split(left * (ratio / column_norm)), right_parts, 1, 1).astype(update_ref.dtype)
    me = pl.multiple_of(lax.axis_index("fsdp") * 8, 8)
    basis_ref[...] = right[pl.ds(me, 8), :] / column_norm

    def sent_y(d):
        done(gown, s_gy.at[d])
        done(norms.at[y], s_n.at[d])

    def sent_x(d):
        done(gxsum.at[x_of(d)], s_hx.at[d])
        for k in blocks:
            done(upper(k, x, core), s_gx.at[d * len(blocks) + k])
        done(wxsum.at[x_of(d)], s_x.at[d])

    def sent_z(d):
        done(gzsum, s_hz.at[d])
        done(wzsum.at[z_of(d)], s_z.at[d])
        done(wown, s_wz.at[d])

    each(1, ys_n, sent_y)
    each(1, XS, sent_x)
    each(1, zs_n, sent_z)
    each(0, XS, lambda d: done(wpart.at[:, x_of(d), 1 - core], s_c.at[d]))
    done(ghalf, s_hc)
    for k in blocks:
        done(upper(k, slice(None), core), s_gc.at[k])
    for step, piece, rows, way, sign, steps in hops():
        k = sem(way, step, piece)
        done(part.at[y, rows], s_y.at[k])
        done(chunks.at[y, rows], s_y2.at[k])
    for k in range(XS):
        done(w_at(x) if k < 2 else w_at(x, halves[k - 2]), s_wx.at[k])
        done(w_at(k), s_wc.at[k])


def on_device(momentum, gradient, right_basis):
    rows, cols = momentum.shape
    rank = right_basis.shape[1]
    groups = lax.axis_size("fsdp")
    ys_n = lax.axis_size("tensor")
    zs_n = groups // (XS * CORES)
    total_rows = rows * groups
    ratio = math.sqrt(total_rows / (cols * ys_n))
    f32 = jnp.float32
    lanes = 128
    half = rows * rank // (ys_n * lanes)
    per = lanes * ys_n // rank

    def buffer(*shape):
        return pltpu.VMEM(shape, f32)

    one = [pltpu.SemaphoreType.DMA] * 2

    def sems(n):
        return [pltpu.SemaphoreType.DMA((n,))] * 2

    gsum = buffer(XS, 8, rank)
    wsum = buffer(XS, zs_n, 8, rank)
    vmem = pl.BlockSpec(memory_space=pltpu.VMEM)
    return pl.pallas_call(
        functools.partial(kernel, zs_n, ys_n, total_rows, ratio),
        name="step",
        out_shape=(
            jax.ShapeDtypeStruct((rows, cols), jnp.bfloat16),
            jax.ShapeDtypeStruct((rows, cols), f32),
            jax.ShapeDtypeStruct((rows, rank), f32),
            jax.ShapeDtypeStruct((8, rank), f32),
        ),
        in_specs=[pl.BlockSpec(memory_space=pltpu.HBM)] * 3,
        out_specs=(vmem,) * 4,
        scratch_shapes=[
            buffer(rows, cols), pltpu.VMEM((rows, cols), jnp.bfloat16), buffer(cols, rank), pltpu.SemaphoreType.DMA((3,)),
            buffer(ys_n, half, lanes), buffer(ys_n, half, lanes), buffer(ys_n, half, lanes), buffer(ys_n, half, lanes),
            buffer(rows, rank),
            buffer(per, XS, CORES, 8, rank), gsum, gsum, gsum, buffer(8, rank), buffer(zs_n, 8, rank),
            buffer(ys_n, XS, CORES, 8, rank),
            buffer(zs_n, XS, CORES, 8, rank), wsum, wsum, wsum, buffer(zs_n, 8, rank), buffer(zs_n, 8, rank),
            buffer(zs_n, XS, CORES, 8, rank),
            buffer(rank, rank), buffer(BLOCK, BLOCK), buffer(8 * GROUP, BLOCK), buffer(cols, rank), buffer(ys_n, 1, rank),
            *sems(2 * ys_n), *sems(2 * ys_n), *sems(ys_n),
            *one, *sems(XS), *sems(zs_n), *sems(ys_n), *sems(XS * rank // lanes), *sems(rank // lanes),
            *sems(XS), *sems(XS), *sems(zs_n), *sems(zs_n), *sems(XS), *sems(XS),
        ],
        compiler_params=pltpu.CompilerParams(
            collective_id=0, has_side_effects=True, vmem_limit_bytes=VMEM_LIMIT
        ),
    )(momentum, gradient, right_basis)


def solution(mesh):
    in_specs = (P("fsdp", "tensor"), P("fsdp", "tensor"), P("tensor", None))
    out_specs = (
        P("fsdp", "tensor"),
        P("fsdp", "tensor"),
        P("fsdp", None),
        P(("tensor", "fsdp"), None),
    )
    return jax.shard_map(
        on_device, mesh=mesh, in_specs=in_specs, out_specs=out_specs, check_vma=False
    )
```

```python
import functools
import math

import jax
import jax.numpy as jnp
from jax import lax
from jax.experimental import pallas as pl
from jax.experimental.pallas import tpu as pltpu
from jax.sharding import PartitionSpec as P

EPSILON = 1e-06
HIGHEST = lax.Precision.HIGHEST
MESH = pl.DeviceIdType.MESH
XS, CORES = 4, 2
VMEM_LIMIT = 24 * 1024 * 1024


def dot(a, b, lhs=1, rhs=0):
    return lax.dot_general(
        a, b, (((lhs,), (rhs,)), ((), ())), precision=HIGHEST, preferred_element_type=jnp.float32
    )


def split(a):
    high = a.astype(jnp.bfloat16)
    return high, (a - high.astype(jnp.float32)).astype(jnp.bfloat16)


def dot3(a, b, lhs=1, rhs=0):
    def one(p, q):
        return lax.dot_general(p, q, (((lhs,), (rhs,)), ((), ())), preferred_element_type=jnp.float32)

    return one(a[0], b[0]) + (one(a[0], b[1]) + one(a[1], b[0]))


def place():
    f = lax.axis_index("fsdp")
    y = lax.axis_index("tensor")
    return f // (XS * CORES), (f // CORES) % XS, f % CORES, y


def device(z, x, core, y):
    return ((z * XS + x) * CORES + core, y)


def each(start, stop, body):
    def step(i, carry):
        body(i)
        return carry

    lax.fori_loop(start, stop, step, 0)


def far_first(count):
    return sorted(range(1, count), key=lambda d: -min(d, count - d))


BLOCK = 128
GROUP, NEAR = 4, 1


def factor_block(tiles, panel_ref):
    shape = (8, BLOCK)
    lane = lax.broadcasted_iota(jnp.int32, shape, 1)
    sub = lax.broadcasted_iota(jnp.int32, shape, 0)
    count = len(tiles)
    out = []

    def column(tile, k):
        return jnp.broadcast_to(tile[:, k : k + 1], shape)

    def row(tile, k):
        return jnp.broadcast_to(tile[k : k + 1, :], shape)

    tiles = list(tiles)
    for t in range(count):
        base = 8 * t
        first = t // GROUP * GROUP
        end = first + GROUP
        near = min(end + NEAR, count)
        here = (lane >= base) & (lane < base + 8)
        tile = tiles[t]
        cols = [column(tile, base + c) for c in range(8)]
        start = jnp.where(here, jnp.where(lane - base == sub, 1.0, 0.0), tile)
        scale, rows, low = [], [], {}
        for p in range(8):
            r = row(lax.rsqrt(cols[p]), p)
            lp = cols[p] * r
            for c in range(p + 1, 8):
                low[p, c] = row(lp, c)
                cols[c] = cols[c] - lp * low[p, c]
            w = row(start, p)
            for q in range(p):
                w = w - low[q, p] * rows[q]
            rows.append(w * r)
            scale.append(r)
        done = rows[7]
        for p in range(7):
            done = jnp.where(sub == p, rows[p], done)
        out.append(jnp.where(lane < base + 8, done, 0.0))
        panel_ref[base - 8 * first : base - 8 * first + 8, :] = jnp.where((lane < base + 8) | (lane >= 8 * end), done, 0.0)
        if t + 1 == count:
            break
        solved = [None] * 8
        for p in reversed(range(8)):
            w = rows[p]
            for q in reversed(range(p + 1, 8)):
                w = w - low[p, q] * solved[q]
            solved[p] = w * scale[p]
        for i in range(t + 1, near):
            acc = jnp.where(here, 0.0, tiles[i])
            for p in reversed(range(8)):
                acc = acc - column(tiles[i], base + p) * solved[p]
            tiles[i] = acc
        if t + 1 == end and near < count:
            panel = panel_ref[...]
            low = jnp.where(lax.broadcasted_iota(jnp.int32, panel.shape, 1) >= 8 * near, panel, 0.0)
            change = dot3(split(low), split(panel), 0, 0)
            gone = (lane >= 8 * first) & (lane < 8 * end)
            for i in range(near, count):
                tiles[i] = jnp.where(gone, 0.0, tiles[i]) - change[8 * i : 8 * i + 8]
    return out


def factor_step(b, work, top_ref, panel_ref, between):
    size = work.shape[0]
    off = pl.multiple_of(b * BLOCK, BLOCK)
    here = pl.ds(off, BLOCK)
    tiles = [work[pl.ds(pl.multiple_of(off + 8 * i, 8), 8), here] for i in range(BLOCK // 8)]
    for i, tile in enumerate(factor_block(tiles, panel_ref)):
        top_ref[8 * i : 8 * i + 8, :] = tile
    between()
    lane = lax.broadcasted_iota(jnp.int32, (BLOCK, size), 1)
    top = top_ref[...]
    inverse = split(top)
    panel = dot3(inverse, split(work[here, :]))
    work[here, :] = jnp.where(lane < off, panel, 0.0)
    work[here, here] = top

    @pl.when(b + 1 < size // BLOCK)
    def _():
        after = jnp.where(lane >= off + BLOCK, panel, 0.0)
        shape = (size - BLOCK, size)
        below = lax.broadcasted_iota(jnp.int32, shape, 0) >= off
        lanes = lax.broadcasted_iota(jnp.int32, shape, 1)
        gone = below & (lanes >= off) & (lanes < off + BLOCK)
        row = work[here, :] + after
        work[BLOCK:, :] = jnp.where(gone, 0.0, work[BLOCK:, :]) - dot3(split(after[:, BLOCK:]), split(row), 0, 0)


def kernel(
    zs_n, ys_n, total_rows, ratio, m_hbm, g_hbm, q_hbm, update_ref, momentum_ref, left_ref, basis_ref,
    m_ref, g_ref, q_ref, s_in, part, ybuf, ysum, chunks, raw, gpart, gcbuf, gxsum, gxbuf, gzsum, gzbuf, gfull,
    wpart, wcbuf, wxsum, wxbuf, wzsum, wzbuf, wfull, work, top, panel, right, norms,
    s_y, r_y, s_y2, r_y2, s_n, r_n,
    s_hc, r_hc, s_hx, r_hx, s_hz, r_hz, s_gy, r_gy, s_gx, r_gx, s_gc, r_gc,
    s_c, r_c, s_x, r_x, s_z, r_z, s_wz, r_wz, s_wx, r_wx, s_wc, r_wc,
):
    loads = [
        pltpu.make_async_copy(src, dst, s_in.at[k])
        for k, (src, dst) in enumerate(((q_hbm, q_ref), (m_hbm, m_ref), (g_hbm, g_ref)))
    ]
    for load in loads:
        load.start()
    z, x, core, y = place()
    half = part.shape[1]
    lanes = part.shape[2]
    rank = raw.shape[1]
    across = rank // lanes

    def send(src, dst, ssem, rsem, to):
        pltpu.make_async_remote_copy(
            src_ref=src, dst_ref=dst, send_sem=ssem, recv_sem=rsem, device_id=to, device_id_type=MESH
        ).start()

    def done(ref, sem):
        pltpu.make_async_copy(ref, ref, sem).wait()

    def total(ref):
        acc = ref[0]
        for k in range(1, ref.shape[0]):
            acc = acc + ref[k]
        return acc

    def ring(at, count):
        known = [at] + [lax.rem(at + d, count) for d in range(1, count)]
        return lambda d: known[d] if isinstance(d, int) else lax.rem(at + d, count)

    x_of, y_of, z_of = ring(x, XS), ring(y, ys_n), ring(z, zs_n)

    def at_x(k):
        return device(z, k, core, y)

    def at_y(k):
        return device(z, x, core, k)

    def at_z(k):
        return device(k, x, core, y)

    partner = device(z, x, 1 - core, y)
    barrier = pltpu.get_barrier_semaphore()

    def greet(to):
        pl.semaphore_signal(barrier, inc=1, device_id=to, device_id_type=MESH)

    each(1, ys_n, lambda d: greet(at_y(y_of(d))))
    greet(partner)
    each(1, XS, lambda d: greet(at_x(x_of(d))))
    each(1, zs_n, lambda d: greet(at_z(z_of(d))))

    for load in loads:
        load.wait()
    m_ref[...] = m_ref[...] + g_ref[...].astype(jnp.float32)
    summed = split(m_ref[...])
    left_part = dot3(summed, split(q_ref[...]))
    for k in range(ys_n):
        row, col = k // across, k % across
        part[k] = left_part[row * half : (row + 1) * half, col * lanes : (col + 1) * lanes]
    pl.semaphore_wait(barrier, (ys_n - 1) + 1 + (XS - 1) + (zs_n - 1))

    ways = ((1, ys_n // 2), (-1, (ys_n - 1) // 2))
    most = ways[0][1]
    cut = half // 16 * 8 + 8
    pieces = (slice(0, cut), slice(cut, half))

    def slot(way, step):
        return way * most + step - 1

    def sem(way, step, piece):
        return slot(way, step) * len(pieces) + piece

    def hops():
        for step in range(1, most + 1):
            for piece, rows in enumerate(pieces):
                for way, (sign, steps) in enumerate(ways):
                    if step <= steps:
                        yield step, piece, rows, way, sign * (1 - 2 * piece), steps

    for step, piece, rows, way, sign, steps in hops():
        to = y_of((sign * (steps + 1 - step)) % ys_n)
        out = part.at[to, rows]
        if step > 1:
            came = slot(way, step - 1)
            done(ybuf.at[came, rows], r_y.at[sem(way, step - 1, piece)])
            ysum[came + 1, rows] = ybuf[came, rows] + part[to, rows]
            out = ysum.at[came + 1, rows]
        k = sem(way, step, piece)
        send(out, ybuf.at[slot(way, step), rows], s_y.at[k], r_y.at[k], at_y(y_of(sign % ys_n)))
    for piece, rows in enumerate(pieces):
        acc = part[y, rows]
        for way, (sign, steps) in enumerate(ways):
            done(ybuf.at[slot(way, steps), rows], r_y.at[sem(way, steps, piece)])
            acc = acc + ybuf[slot(way, steps), rows]
        chunks[y, rows] = acc
    for step, piece, rows, way, sign, steps in hops():
        block = chunks.at[y_of((-sign * (step - 1)) % ys_n), rows]
        if step > 1:
            done(block, r_y2.at[sem(way, step - 1, piece)])
        k = sem(way, step, piece)
        send(block, block, s_y2.at[k], r_y2.at[k], at_y(y_of(sign % ys_n)))
    for piece, rows in enumerate(pieces):
        for way, (sign, steps) in enumerate(ways):
            done(chunks.at[y_of((-sign * (1 - 2 * piece) * steps) % ys_n), rows], r_y2.at[sem(way, steps, piece)])
    for k in range(ys_n):
        row, col = k // across, k % across
        raw[row * half : (row + 1) * half, col * lanes : (col + 1) * lanes] = chunks[k]

    per = gpart.shape[0]
    pair = raw[:, pl.ds(pl.multiple_of((y // per) * 128, 128), 128)]
    gpart[...] = dot(pair, raw[...], 0, 0).reshape(gpart.shape)
    plane = y % per
    ghalf = gpart.at[plane, :, 1 - core]
    send(ghalf, gcbuf, s_hc, r_hc, partner)

    wpart[...] = dot3(summed, split(raw[...]), 0, 0).reshape(wpart.shape)

    def w_across(d):
        send(wpart.at[:, x_of(d), 1 - core], wcbuf.at[x_of(d)], s_c.at[d], r_c.at[x_of(d)], partner)

    for d in far_first(XS):
        w_across(d)
    w_across(0)

    done(gcbuf, r_hc)
    gxsum[...] = gpart[plane, :, core] + gcbuf[...]
    for d in far_first(XS):
        send(gxsum.at[x_of(d)], gxbuf.at[x], s_hx.at[d], r_hx.at[x], at_x(x_of(d)))
    gxbuf[x] = gxsum[x]

    def w_forward(d):
        k = x_of(d)
        done(wcbuf.at[k], r_c.at[k])
        wxsum[k] = wpart[:, k, core] + wcbuf[k]
        send(wxsum.at[k], wxbuf.at[x], s_x.at[d], r_x.at[x], at_x(k))

    for d in far_first(XS):
        w_forward(d)
    for d in range(1, XS):
        done(gxbuf.at[x_of(d)], r_hx.at[x_of(d)])
    gzsum[...] = total(gxbuf)
    for d in far_first(zs_n):
        send(gzsum, gzbuf.at[z], s_hz.at[d], r_hz.at[z], at_z(z_of(d)))
    gzbuf[z] = gzsum[...]
    done(wcbuf.at[x], r_c.at[x])
    wxbuf[x] = wpart[:, x, core] + wcbuf[x]

    for d in range(1, zs_n):
        done(gzbuf.at[z_of(d)], r_hz.at[z_of(d)])
    gfull[y, x, core] = total(gzbuf)
    gown = gfull.at[y, x, core]
    for d in far_first(ys_n):
        send(gown, gown, s_gy.at[d], r_gy.at[y], at_y(y_of(d)))

    for d in range(1, XS):
        done(wxbuf.at[x_of(d)], r_x.at[x_of(d)])
    wzsum[...] = total(wxbuf)
    for d in far_first(zs_n):
        send(wzsum.at[z_of(d)], wzbuf.at[z], s_z.at[d], r_z.at[z], at_z(z_of(d)))
    wzbuf[z] = wzsum[z]

    for d in range(1, ys_n):
        done(gfull.at[y_of(d), x, core], r_gy.at[y_of(d)])
    blocks = range(rank // lanes)

    def upper(block, *at):
        return gfull.at[(slice(0, per * (block + 1)), *at, slice(None), slice(block * lanes, (block + 1) * lanes))]

    def gather_x(d):
        for k in blocks:
            mine = upper(k, x, core)
            send(mine, mine, s_gx.at[d * len(blocks) + k], r_gx.at[x * len(blocks) + k], at_x(x_of(d)))

    def gathered_x(d):
        for k in blocks:
            done(upper(k, x_of(d), core), r_gx.at[x_of(d) * len(blocks) + k])

    for d in far_first(XS):
        gather_x(d)
    for d in range(1, XS):
        gathered_x(d)
    for k in blocks:
        send(upper(k, slice(None), core), upper(k, slice(None), core), s_gc.at[k], r_gc.at[k], partner)
    for d in range(1, zs_n):
        done(wzbuf.at[z_of(d)], r_z.at[z_of(d)])
    wfull[z, x, core] = total(wzbuf)
    wown = wfull.at[z, x, core]
    for d in far_first(zs_n):
        send(wown, wown, s_wz.at[d], r_wz.at[z], at_z(z_of(d)))
    for k in blocks:
        done(upper(k, slice(None), 1 - core), r_gc.at[k])
        end = (k + 1) * lanes
        here = slice(k * lanes, end)
        work[0:end, here] = gfull[0 : per * (k + 1), :, :, :, here].reshape(end, lanes)
        if end < rank:
            work[end:, here] = jnp.zeros((rank - end, lanes), jnp.float32)

    cutz = zs_n // 2
    halves = (slice(0, cutz), slice(cutz, zs_n))

    def w_at(k, zs=slice(None)):
        return wfull.at[zs, k, core]

    def w_core(k):
        send(w_at(k), w_at(k), s_wc.at[k], r_wc.at[k], partner)

    def w_start():
        for d in range(1, zs_n):
            done(wfull.at[z_of(d), x, core], r_wz.at[z_of(d)])
        send(w_at(x), w_at(x), s_wx.at[0], r_wx.at[0], at_x(x_of(1)))
        send(w_at(x), w_at(x), s_wx.at[1], r_wx.at[1], at_x(x_of(XS - 1)))
        w_core(x)

    def w_relay():
        behind, ahead = w_at(x_of(XS - 1), halves[0]), w_at(x_of(1), halves[1])
        done(w_at(x_of(XS - 1)), r_wx.at[0])
        send(behind, behind, s_wx.at[2], r_wx.at[2], at_x(x_of(1)))
        done(w_at(x_of(1)), r_wx.at[1])
        send(ahead, ahead, s_wx.at[3], r_wx.at[3], at_x(x_of(XS - 1)))
        w_core(x_of(1))
        w_core(x_of(XS - 1))

    @pl.loop(0, work.shape[0] // BLOCK)
    def _(b):
        def between():
            pl.when(b == 2)(w_start)

        factor_step(b, work, top, panel, between)

    w_relay()
    for k, zs in enumerate(halves):
        done(w_at(x_of(2), zs), r_wx.at[2 + k])
    w_core(x_of(2))

    inverse = split(work[...])
    left = dot3(split(raw[...]), inverse, 1, 1)
    left_ref[...] = left * math.sqrt(total_rows)
    for d in range(XS):
        done(wfull.at[:, x_of(d), 1 - core], r_wc.at[x_of(d)])
    right[...] = dot3(split(wfull[...].reshape(right.shape)), inverse, 1, 1)
    values = right[...]
    norms[y] = jnp.sum(values * values, axis=0, keepdims=True)
    for d in far_first(ys_n):
        send(norms.at[y], norms.at[y], s_n.at[d], r_n.at[y], at_y(y_of(d)))
    right_parts = split(values)
    product = dot3(split(left), right_parts, 1, 1)
    momentum_ref[...] = m_ref[...] - 0.5 * product
    for d in range(1, ys_n):
        done(norms.at[y_of(d)], r_n.at[y_of(d)])
    column_norm = jnp.sqrt(total(norms) + EPSILON)
    update_ref[...] = dot3(split(left * (ratio / column_norm)), right_parts, 1, 1).astype(update_ref.dtype)
    me = pl.multiple_of(lax.axis_index("fsdp") * 8, 8)
    basis_ref[...] = right[pl.ds(me, 8), :] / column_norm

    def sent_y(d):
        done(gown, s_gy.at[d])
        done(norms.at[y], s_n.at[d])

    def sent_x(d):
        done(gxsum.at[x_of(d)], s_hx.at[d])
        for k in blocks:
            done(upper(k, x, core), s_gx.at[d * len(blocks) + k])
        done(wxsum.at[x_of(d)], s_x.at[d])

    def sent_z(d):
        done(gzsum, s_hz.at[d])
        done(wzsum.at[z_of(d)], s_z.at[d])
        done(wown, s_wz.at[d])

    each(1, ys_n, sent_y)
    each(1, XS, sent_x)
    each(1, zs_n, sent_z)
    each(0, XS, lambda d: done(wpart.at[:, x_of(d), 1 - core], s_c.at[d]))
    done(ghalf, s_hc)
    for k in blocks:
        done(upper(k, slice(None), core), s_gc.at[k])
    for step, piece, rows, way, sign, steps in hops():
        k = sem(way, step, piece)
        done(part.at[y, rows], s_y.at[k])
        done(chunks.at[y, rows], s_y2.at[k])
    for k in range(XS):
        done(w_at(x) if k < 2 else w_at(x, halves[k - 2]), s_wx.at[k])
        done(w_at(k), s_wc.at[k])


def on_device(momentum, gradient, right_basis):
    rows, cols = momentum.shape
    rank = right_basis.shape[1]
    groups = lax.axis_size("fsdp")
    ys_n = lax.axis_size("tensor")
    zs_n = groups // (XS * CORES)
    total_rows = rows * groups
    ratio = math.sqrt(total_rows / (cols * ys_n))
    f32 = jnp.float32
    lanes = 128
    half = rows * rank // (ys_n * lanes)
    per = lanes * ys_n // rank

    def buffer(*shape):
        return pltpu.VMEM(shape, f32)

    one = [pltpu.SemaphoreType.DMA] * 2

    def sems(n):
        return [pltpu.SemaphoreType.DMA((n,))] * 2

    gsum = buffer(XS, 8, rank)
    wsum = buffer(XS, zs_n, 8, rank)
    vmem = pl.BlockSpec(memory_space=pltpu.VMEM)
    return pl.pallas_call(
        functools.partial(kernel, zs_n, ys_n, total_rows, ratio),
        name="step",
        out_shape=(
            jax.ShapeDtypeStruct((rows, cols), jnp.bfloat16),
            jax.ShapeDtypeStruct((rows, cols), f32),
            jax.ShapeDtypeStruct((rows, rank), f32),
            jax.ShapeDtypeStruct((8, rank), f32),
        ),
        in_specs=[pl.BlockSpec(memory_space=pltpu.HBM)] * 3,
        out_specs=(vmem,) * 4,
        scratch_shapes=[
            buffer(rows, cols), pltpu.VMEM((rows, cols), jnp.bfloat16), buffer(cols, rank), pltpu.SemaphoreType.DMA((3,)),
            buffer(ys_n, half, lanes), buffer(ys_n, half, lanes), buffer(ys_n, half, lanes), buffer(ys_n, half, lanes),
            buffer(rows, rank),
            buffer(per, XS, CORES, 8, rank), gsum, gsum, gsum, buffer(8, rank), buffer(zs_n, 8, rank),
            buffer(ys_n, XS, CORES, 8, rank),
            buffer(zs_n, XS, CORES, 8, rank), wsum, wsum, wsum, buffer(zs_n, 8, rank), buffer(zs_n, 8, rank),
            buffer(zs_n, XS, CORES, 8, rank),
            buffer(rank, rank), buffer(BLOCK, BLOCK), buffer(8 * GROUP, BLOCK), buffer(cols, rank), buffer(ys_n, 1, rank),
            *sems(2 * ys_n), *sems(2 * ys_n), *sems(ys_n),
            *one, *sems(XS), *sems(zs_n), *sems(ys_n), *sems(XS * rank // lanes), *sems(rank // lanes),
            *sems(XS), *sems(XS), *sems(zs_n), *sems(zs_n), *sems(XS), *sems(XS),
        ],
        compiler_params=pltpu.CompilerParams(
            collective_id=0, has_side_effects=True, vmem_limit_bytes=VMEM_LIMIT
        ),
    )(momentum, gradient, right_basis)


def solution(mesh):
    in_specs = (P("fsdp", "tensor"), P("fsdp", "tensor"), P("tensor", None))
    out_specs = (
        P("fsdp", "tensor"),
        P("fsdp", "tensor"),
        P("fsdp", None),
        P(("tensor", "fsdp"), None),
    )
    return jax.shard_map(
        on_device, mesh=mesh, in_specs=in_specs, out_specs=out_specs, check_vma=False
    )
```
